32 devices in a mesh: clips: 2 (over y), frame: 4 (over z), row: 2 (over x), head: 2 (over core).
Axes of the slice: x: 2, y: 2, z: 4, core: 2. Of those that a mesh axis runs over, the one named last changes fastest.
Arguments:
- query: bfloat16 [64, 16, 8, 1536], P(('clips', 'frame'), 'row', None, 'head'), parts along dimension 0, may hold values from -7 to 7
- keys: bfloat16 [64, 16, 8, 1536], P(('clips', 'frame'), 'row', None, 'head'), parts along dimension 0, may hold values from -6 to 6
- values: bfloat16 [64, 16, 8, 1536], P(('clips', 'frame'), 'row', None, 'head'), parts along dimension 0, may hold values from -6 to 6
Outputs:
- attended: bfloat16 [64, 16, 8, 1536], P(('clips', 'frame'), 'row', None, 'head'), parts along dimension 0
The draws below stay inside these ranges and needn't reach their ends.
There are 2 independent parts, one for each index of `clips`. The reference program is written for one: setup_inputs(seed, part) draws one part's arguments, and reference() takes and returns one part's arrays. A program takes and returns all parts, laid end to end along the dimension named above; each array names one. Nothing has to cross between parts.
All inputs are finite; a program needn't handle non-finite values.
Results may differ from the reference program's by a relative error of at most 0.0047.
Values may be sent and summed in bfloat16 or wider, within the bound.
A program may use at most 64 MiB of HBM per device.

```python
import math
import jax
import jax.numpy as jnp
from jax import lax

HEADS = 12
HD = 128
TF = 4
TR = 8
TC = 8
LATENT_FRAMES = 32
ROWS = 16
COLS = 8


def draw_query(key, part):
    full_shape = (LATENT_FRAMES, ROWS, COLS, HEADS * HD)
    result_values = jnp.clip(jax.random.normal(jax.random.fold_in(key, 21), full_shape, jnp.float32), -6.0, 6.0)
    return result_values.astype(jnp.bfloat16)


def draw_keys(key, part):
    full_shape = (LATENT_FRAMES, ROWS, COLS, HEADS * HD)
    result_values = jnp.clip(jax.random.normal(jax.random.fold_in(key, 31), full_shape, jnp.float32), -6.0, 6.0)
    return result_values.astype(jnp.bfloat16)


def shard_levels(own_key, shape, split, least, largest):
    loudness = 1.0
    for dim, parts in split:
        heights = jax.random.uniform(jax.random.fold_in(jax.random.fold_in(own_key, 6), dim), (parts,), jnp.float32, least / len(split), largest / len(split))
        loudness = loudness * jnp.repeat(jnp.exp(heights), shape[dim] // parts).reshape((-1,) + (1,) * (len(shape) - 1 - dim))
    return loudness


def noise(own_key, extent, width, bound, shards=(), kind=jnp.bfloat16):
    values = jax.random.normal(own_key, extent, jnp.float32) * width
    if len(shards) > 0:
        values = shard_levels(own_key, extent, shards, -0.22, 0.18) * values
    return jnp.clip(values, min=-bound, max=bound).astype(kind)


def setup_inputs(seed: int = 0, part: int = 0) -> dict:
    arg_keys = jax.random.split(jax.random.key(seed), 4)
    part_splits = jax.random.split(jax.random.fold_in(arg_keys[3], part), 4)
    return {
        "query": draw_query(jax.random.fold_in(jax.random.fold_in(arg_keys[3], part), 71), part),
        "keys": draw_keys(jax.random.fold_in(jax.random.fold_in(arg_keys[3], part), 71), part),
        "values": noise(part_splits[2], (LATENT_FRAMES, ROWS, COLS, HEADS * HD), 1.0, 6.0, ((0, 4), (1, 2), (3, 2))),
    }


def reference(query, keys, values):
    frames, rows, columns, features = query.shape
    heads = features // HD
    frame_tiles = frames // TF
    row_tiles = rows // TR
    column_tiles = columns // TC
    tile_size = TF * TR * TC
    score_scale = 1.0 / math.sqrt(HD)

    def tiled(array):
        shaped = array.reshape(frame_tiles, TF, row_tiles, TR, column_tiles, TC, heads, HD)
        shaped = shaped.transpose(0, 2, 4, 1, 3, 5, 6, 7)
        return shaped.reshape(frame_tiles, row_tiles, column_tiles, tile_size, heads, HD)
    padding = ((1, 1), (1, 1), (0, 0), (0, 0), (0, 0), (0, 0))
    tiled_queries = tiled(query)
    key_tiles = jnp.pad(tiled(keys), padding)
    value_tiles = jnp.pad(tiled(values), padding)
    offsets = jnp.arange(3, dtype=jnp.int32) - 1
    block_rows = column_tiles * tile_size

    def one_tile(flat):
        frame_at = (flat // row_tiles).astype(jnp.int32)
        row_at = (flat % row_tiles).astype(jnp.int32)
        zero = jnp.zeros((), jnp.int32)
        starts = (frame_at, row_at, zero, zero, zero, zero)
        query_block = lax.dynamic_slice(tiled_queries, starts, (1, 1, column_tiles, tile_size, heads, HD))
        key_block = lax.dynamic_slice(key_tiles, starts, (3, 3, column_tiles, tile_size, heads, HD))
        value_block = lax.dynamic_slice(value_tiles, starts, (3, 3, column_tiles, tile_size, heads, HD))
        frame_ids = frame_at + offsets
        row_ids = row_at + offsets
        frame_ok = (frame_ids >= 0) & (frame_ids < frame_tiles)
        row_ok = (row_ids >= 0) & (row_ids < row_tiles)
        tile_mask = frame_ok[:, None] & row_ok[None, :]
        allowed = jnp.broadcast_to(tile_mask[None, :, :, None], (block_rows, 3, 3, block_rows))
        allowed = allowed.reshape(block_rows, 9 * block_rows)
        queries = query_block.reshape(block_rows, heads, HD).astype(jnp.float32)
        key_rows = key_block.reshape(-1, heads, HD).astype(jnp.float32)
        value_rows = value_block.reshape(-1, heads, HD).astype(jnp.float32)
        scores = jnp.einsum('qhd,khd->hqk', queries, key_rows) * score_scale
        scores = jnp.where(allowed[None], scores, -jnp.inf)
        row_peak = lax.optimization_barrier(jnp.max(scores, axis=-1, keepdims=True))
        weights = jnp.exp(scores - row_peak)
        row_total = lax.optimization_barrier(jnp.sum(weights, axis=-1, keepdims=True))
        rounded_length = lax.optimization_barrier(weights.astype(jnp.bfloat16)).astype(jnp.float32)
        summed = jnp.einsum('hqk,khd->qhd', rounded_length, value_rows)
        return (summed / jnp.transpose(row_total, (1, 0, 2))).astype(jnp.bfloat16)
    results = lax.map(one_tile, jnp.arange(frame_tiles * row_tiles, dtype=jnp.int32))
    results = results.reshape(frame_tiles, row_tiles, column_tiles, TF, TR, TC, heads, HD)
    results = results.transpose(0, 3, 1, 4, 2, 5, 6, 7)
    return results.reshape(frames, rows, columns, features)
```

```python
import functools
import math

import jax
import jax.numpy as jnp
from jax import lax
from jax.experimental import pallas as pl
from jax.experimental.pallas import tpu as pltpu
from jax.sharding import PartitionSpec as P

HD = 128
TF = 4
TR = 8
TC = 8
MESH = pl.DeviceIdType.MESH


def pair_kernel(
    q_ref,
    k_ref,
    v_ref,
    o_ref,
    qbuf,
    kbuf,
    vbuf,
    obuf,
    local_sem,
    x_send,
    x_recv,
    z_send,
    z_recv,
    o_send,
    o_recv,
    o_local,
    *,
    half,
    tile_frames,
    exponent_scale,
):
    row = lax.axis_index("row")
    frame = lax.axis_index("frame")
    last_frame = lax.axis_size("frame") - 1
    other = 1 - row
    has_prev = frame > 0
    has_next = frame < last_frame

    def columns(side, h):
        return pl.ds(pl.multiple_of((side * half + h) * HD, HD), HD)

    sources = (k_ref, v_ref, q_ref)

    def place(i, h, slot):
        if i == 2:
            return qbuf.at[h, :, slot]
        return (kbuf, vbuf)[i].at[h, 1 : 1 + tile_frames, slot]

    def local_copy(i, h):
        return pltpu.make_async_copy(
            sources[i].at[:, :, columns(row, h)], place(i, h, 0), local_sem.at[i, h]
        )

    def row_copy(i, h):
        return pltpu.make_async_remote_copy(
            sources[i].at[:, :, columns(other, h)],
            place(i, h, 1),
            x_send.at[i, h],
            x_recv.at[i, h],
            device_id={"row": other},
            device_id_type=MESH,
        )

    def frame_copy(i, h, slot, up):
        buf = (kbuf, vbuf)[i]
        edge = tile_frames - 1 if up else 0
        if slot == 0:
            source = sources[i].at[edge, :, columns(row, h)]
        else:
            source = buf.at[h, 1 + edge, 1]
        return pltpu.make_async_remote_copy(
            source,
            buf.at[h, 0 if up else tile_frames + 1, slot],
            z_send.at[slot, i, int(up), h],
            z_recv.at[slot, i, int(up), h],
            device_id={"frame": frame + 1 if up else frame - 1},
            device_id_type=MESH,
        )

    def send_edges(i, h, slot):
        @pl.when(has_next)
        def _():
            frame_copy(i, h, slot, True).start()

        @pl.when(has_prev)
        def _():
            frame_copy(i, h, slot, False).start()

    def receive_edges(i, h, slot):
        @pl.when(has_prev)
        def _():
            frame_copy(i, h, slot, True).wait_recv()

        @pl.when(has_next)
        def _():
            frame_copy(i, h, slot, False).wait_recv()

    def finish_edges(i, h, slot):
        @pl.when(has_next)
        def _():
            frame_copy(i, h, slot, True).wait_send()

        @pl.when(has_prev)
        def _():
            frame_copy(i, h, slot, False).wait_send()

    def return_copy(h, j, side):
        return pltpu.make_async_remote_copy(
            obuf.at[h, j, 1],
            o_ref.at[j, :, columns(side, h)],
            o_send.at[h, j],
            o_recv.at[h, j],
            device_id={"row": other},
            device_id_type=MESH,
        )

    def keep_copy(h, j):
        return pltpu.make_async_copy(
            obuf.at[h, j, 0], o_ref.at[j, :, columns(row, h)], o_local.at[h, j]
        )

    barrier = pltpu.get_barrier_semaphore()
    pl.semaphore_signal(barrier, inc=1, device_id={"row": other}, device_id_type=MESH)

    @pl.when(has_next)
    def _():
        pl.semaphore_signal(barrier, inc=1, device_id={"frame": frame + 1}, device_id_type=MESH)

    @pl.when(has_prev)
    def _():
        pl.semaphore_signal(barrier, inc=1, device_id={"frame": frame - 1}, device_id_type=MESH)

    pl.semaphore_wait(barrier, 1 + has_prev.astype(jnp.int32) + has_next.astype(jnp.int32))

    @pl.loop(0, half)
    def _(h):
        for i in range(3):
            row_copy(i, h).start()

    @pl.loop(0, half)
    def _(h):
        for i in range(2):
            send_edges(i, h, 0)
        for i in range(3):
            local_copy(i, h).start()

    def attend(h, slot, j, first, count):
        q = qbuf[h, j, slot]
        k = kbuf[h, pl.ds(first, count)].reshape(-1, HD)
        v = vbuf[h, pl.ds(first, count)].reshape(-1, HD)
        s = lax.dot_general(q, k, (((1,), (1,)), ((), ())), preferred_element_type=jnp.float32)
        m = jnp.max(s, axis=1, keepdims=True)
        p = jnp.exp2((s - m) * exponent_scale)
        l = jnp.sum(p, axis=1, keepdims=True)
        o = jnp.dot(p.astype(jnp.bfloat16), v, preferred_element_type=jnp.float32)
        obuf[h, j, slot] = (o / l).astype(obuf.dtype)

    @pl.loop(0, half)
    def _(h):
        for i in range(2):
            row_copy(i, h).wait_recv()
            send_edges(i, h, 1)
        row_copy(2, h).wait_recv()
        for i in range(3):
            local_copy(i, h).wait()
        for i in range(2):
            for slot in range(2):
                receive_edges(i, h, slot)

        @pl.loop(0, 2 * tile_frames)
        def _(t):
            j = lax.rem(t, tile_frames)
            slot = 1 - t // tile_frames
            below = jnp.logical_or(has_prev, j > 0)
            above = jnp.logical_or(has_next, j < tile_frames - 1)

            @pl.when(jnp.logical_and(below, above))
            def _():
                attend(h, slot, j, j, 3)

            @pl.when(jnp.logical_not(jnp.logical_and(below, above)))
            def _():
                attend(h, slot, j, jnp.where(below, j, j + 1), 2)

            @pl.when(slot == 1)
            def _():
                return_copy(h, j, row).start()

            @pl.when(slot == 0)
            def _():
                keep_copy(h, j).start()

    @pl.loop(0, half)
    def _(h):
        for i in range(3):
            row_copy(i, h).wait_send()
        for i in range(2):
            for slot in range(2):
                finish_edges(i, h, slot)
        for j in range(tile_frames):
            keep_copy(h, j).wait()
            return_copy(h, j, row).wait_send()

    @pl.loop(0, half)
    def _(h):
        for j in range(tile_frames):
            return_copy(h, j, other).wait_recv()


def pair_attention(query, keys, values):
    tile_frames, tile_size, features = query.shape
    half = features // HD // 2
    kernel = functools.partial(
        pair_kernel,
        half=half,
        tile_frames=tile_frames,
        exponent_scale=math.log2(math.e) / math.sqrt(HD),
    )
    window = (half, tile_frames + 2, 2, tile_size, HD)
    own = (half, tile_frames, 2, tile_size, HD)
    dma = pltpu.SemaphoreType.DMA
    return pl.pallas_call(
        kernel,
        out_shape=jax.ShapeDtypeStruct(query.shape, query.dtype),
        in_specs=[pl.BlockSpec(memory_space=pltpu.HBM)] * 3,
        out_specs=pl.BlockSpec(memory_space=pltpu.VMEM),
        scratch_shapes=[
            pltpu.VMEM(own, query.dtype),
            pltpu.VMEM(window, keys.dtype),
            pltpu.VMEM(window, values.dtype),
            pltpu.VMEM(own, query.dtype),
            dma((3, half)),
            dma((3, half)),
            dma((3, half)),
            dma((2, 2, 2, half)),
            dma((2, 2, 2, half)),
            dma((half, tile_frames)),
            dma((half, tile_frames)),
            dma((half, tile_frames)),
        ],
        compiler_params=pltpu.CompilerParams(
            collective_id=0, has_side_effects=True, vmem_limit_bytes=61000 * 1024
        ),
    )(query, keys, values)


def shift(cells, axis, forward):
    count = lax.axis_size(axis)
    if forward:
        pairs = [(i, i + 1) for i in range(count - 1)]
    else:
        pairs = [(i + 1, i) for i in range(count - 1)]
    return lax.ppermute(cells, axis, pairs)


def attention_kernel(bias_ref, q_ref, k_ref, v_ref, o_ref, *, tile_frames, score_scale):
    for j in range(tile_frames):
        q = q_ref[j]
        k = k_ref[:, j : j + 3].reshape(-1, HD)
        v = v_ref[:, j : j + 3].reshape(-1, HD)
        s = lax.dot_general(q, k, (((1,), (1,)), ((), ())), preferred_element_type=jnp.float32)
        s = s * score_scale + bias_ref[j]
        m = jnp.max(s, axis=1, keepdims=True)
        p = jnp.exp(s - m)
        l = jnp.sum(p, axis=1, keepdims=True)
        o = jnp.dot(p.astype(jnp.bfloat16), v, preferred_element_type=jnp.float32)
        o_ref[j] = (o / l).astype(o_ref.dtype)


def per_device(query, keys, values):
    frames, rows, columns, features = query.shape
    tile_frames = frames // TF
    tile_size = TF * TR * TC
    heads_here = features // HD
    score_scale = 1.0 / math.sqrt(HD)

    def tiles(x):
        return x.reshape(tile_frames, tile_size, features)

    paired = lax.axis_size("row") == 2 and lax.axis_size("frame") > 1
    if paired and heads_here % 2 == 0 and tile_frames > 1:
        out = pair_attention(tiles(query), tiles(keys), tiles(values))
        return out.reshape(query.shape)

    kv = (tiles(keys), tiles(values))
    above = shift(kv, "row", True)
    below = shift(kv, "row", False)
    own_prev = shift(tuple(x[tile_frames - 1] for x in kv), "frame", True)
    own_next = shift(tuple(x[0] for x in kv), "frame", False)
    diag_prev = shift(
        tuple(jnp.stack((a[tile_frames - 1], b[tile_frames - 1])) for a, b in zip(above, below)),
        "frame",
        True,
    )
    diag_next = shift(tuple(jnp.stack((a[0], b[0])) for a, b in zip(above, below)), "frame", False)

    def window(i):
        middle = jnp.concatenate((own_prev[i][None], kv[i], own_next[i][None]), 0)
        top = jnp.concatenate((diag_prev[i][0][None], above[i], diag_next[i][0][None]), 0)
        bottom = jnp.concatenate((diag_prev[i][1][None], below[i], diag_next[i][1][None]), 0)
        return jnp.stack((top, middle, bottom))

    key_window = window(0)
    value_window = window(1)

    frame_index = lax.axis_index("frame")
    row_index = lax.axis_index("row")
    offsets = jnp.arange(3, dtype=jnp.int32) - 1
    global_frames = frame_index * tile_frames + jnp.arange(tile_frames + 2, dtype=jnp.int32) - 1
    frame_ok = (global_frames >= 0) & (global_frames < tile_frames * lax.axis_size("frame"))
    row_ids = row_index + offsets
    row_ok = (row_ids >= 0) & (row_ids < lax.axis_size("row"))
    bias_rows = []
    for j in range(tile_frames):
        ok = row_ok[:, None] & frame_ok[None, j : j + 3]
        ok = jnp.broadcast_to(ok[:, :, None], (3, 3, tile_size)).reshape(1, 9 * tile_size)
        bias_rows.append(jnp.where(ok, 0.0, -jnp.inf).astype(jnp.float32))
    bias = jnp.stack(bias_rows)

    q = tiles(query)
    kernel = functools.partial(
        attention_kernel, tile_frames=tile_frames, score_scale=score_scale
    )
    window_block = (3, tile_frames + 2, tile_size, HD)
    out = pl.pallas_call(
        kernel,
        grid=(heads_here,),
        in_specs=[
            pl.BlockSpec((tile_frames, 1, 9 * tile_size), lambda h: (0, 0, 0)),
            pl.BlockSpec((tile_frames, tile_size, HD), lambda h: (0, 0, h)),
            pl.BlockSpec(window_block, lambda h: (0, 0, 0, h)),
            pl.BlockSpec(window_block, lambda h: (0, 0, 0, h)),
        ],
        out_specs=pl.BlockSpec((tile_frames, tile_size, HD), lambda h: (0, 0, h)),
        out_shape=jax.ShapeDtypeStruct(q.shape, query.dtype),
        compiler_params=pltpu.CompilerParams(vmem_limit_bytes=48 * 1024 * 1024),
    )(bias, q, key_window, value_window)
    return out.reshape(frames, rows, columns, features)


def solution(mesh):
    return jax.shard_map(
        per_device,
        mesh=mesh,
        in_specs=(
            P(("clips", "frame"), "row", None, "head"),
            P(("clips", "frame"), "row", None, "head"),
            P(("clips", "frame"), "row", None, "head"),
        ),
        out_specs=P(("clips", "frame"), "row", None, "head"),
        check_vma=False,
    )
```

```python
import functools
import math

import jax
import jax.numpy as jnp
from jax import lax
from jax.experimental import pallas as pl
from jax.experimental.pallas import tpu as pltpu
from jax.sharding import PartitionSpec as P

HD = 128
TF = 4
TR = 8
TC = 8
MESH = pl.DeviceIdType.MESH


def pair_kernel(
    q_ref,
    k_ref,
    v_ref,
    o_ref,
    qbuf,
    kbuf,
    vbuf,
    obuf,
    local_sem,
    x_send,
    x_recv,
    z_send,
    z_recv,
    o_send,
    o_recv,
    o_local,
    *,
    half,
    tile_frames,
    exponent_scale,
):
    row = lax.axis_index("row")
    frame = lax.axis_index("frame")
    last_frame = lax.axis_size("frame") - 1
    other = 1 - row
    has_prev = frame > 0
    has_next = frame < last_frame

    def columns(side, h):
        return pl.ds(pl.multiple_of((side * half + h) * HD, HD), HD)

    sources = (k_ref, v_ref, q_ref)

    def place(i, h, slot):
        if i == 2:
            return qbuf.at[h, :, slot]
        return (kbuf, vbuf)[i].at[h, 1 : 1 + tile_frames, slot]

    def local_copy(i, h):
        return pltpu.make_async_copy(
            sources[i].at[:, :, columns(row, h)], place(i, h, 0), local_sem.at[i, h]
        )

    def row_copy(i, h):
        return pltpu.make_async_remote_copy(
            sources[i].at[:, :, columns(other, h)],
            place(i, h, 1),
            x_send.at[i, h],
            x_recv.at[i, h],
            device_id={"row": other},
            device_id_type=MESH,
        )

    def frame_copy(i, h, slot, up):
        buf = (kbuf, vbuf)[i]
        edge = tile_frames - 1 if up else 0
        if slot == 0:
            source = sources[i].at[edge, :, columns(row, h)]
        else:
            source = buf.at[h, 1 + edge, 1]
        return pltpu.make_async_remote_copy(
            source,
            buf.at[h, 0 if up else tile_frames + 1, slot],
            z_send.at[slot, i, int(up), h],
            z_recv.at[slot, i, int(up), h],
            device_id={"frame": frame + 1 if up else frame - 1},
            device_id_type=MESH,
        )

    def send_edges(i, h, slot):
        @pl.when(has_next)
        def _():
            frame_copy(i, h, slot, True).start()

        @pl.when(has_prev)
        def _():
            frame_copy(i, h, slot, False).start()

    def receive_edges(i, h, slot):
        @pl.when(has_prev)
        def _():
            frame_copy(i, h, slot, True).wait_recv()

        @pl.when(has_next)
        def _():
            frame_copy(i, h, slot, False).wait_recv()

    def finish_edges(i, h, slot):
        @pl.when(has_next)
        def _():
            frame_copy(i, h, slot, True).wait_send()

        @pl.when(has_prev)
        def _():
            frame_copy(i, h, slot, False).wait_send()

    def return_copy(h, j, side):
        return pltpu.make_async_remote_copy(
            obuf.at[h, j, 1],
            o_ref.at[j, :, columns(side, h)],
            o_send.at[h, j],
            o_recv.at[h, j],
            device_id={"row": other},
            device_id_type=MESH,
        )

    def keep_copy(h, j):
        return pltpu.make_async_copy(
            obuf.at[h, j, 0], o_ref.at[j, :, columns(row, h)], o_local.at[h, j]
        )

    barrier = pltpu.get_barrier_semaphore()
    pl.semaphore_signal(barrier, inc=1, device_id={"row": other}, device_id_type=MESH)

    @pl.when(has_next)
    def _():
        pl.semaphore_signal(barrier, inc=1, device_id={"frame": frame + 1}, device_id_type=MESH)

    @pl.when(has_prev)
    def _():
        pl.semaphore_signal(barrier, inc=1, device_id={"frame": frame - 1}, device_id_type=MESH)

    pl.semaphore_wait(barrier, 1 + has_prev.astype(jnp.int32) + has_next.astype(jnp.int32))

    @pl.loop(0, half)
    def _(h):
        for i in range(3):
            row_copy(i, h).start()

    @pl.loop(0, half)
    def _(h):
        for i in range(2):
            send_edges(i, h, 0)
        for i in range(3):
            local_copy(i, h).start()

    def attend(h, slot, j, first, count):
        q = qbuf[h, j, slot]
        k = kbuf[h, pl.ds(first, count)].reshape(-1, HD)
        v = vbuf[h, pl.ds(first, count)].reshape(-1, HD)
        s = lax.dot_general(q, k, (((1,), (1,)), ((), ())), preferred_element_type=jnp.float32)
        m = jnp.max(s, axis=1, keepdims=True)
        p = jnp.exp2((s - m) * exponent_scale)
        l = jnp.sum(p, axis=1, keepdims=True)
        o = jnp.dot(p.astype(jnp.bfloat16), v, preferred_element_type=jnp.float32)
        obuf[h, j, slot] = (o / l).astype(obuf.dtype)

    @pl.loop(0, half)
    def _(h):
        for i in range(2):
            row_copy(i, h).wait_recv()
            send_edges(i, h, 1)
        row_copy(2, h).wait_recv()
        for i in range(3):
            local_copy(i, h).wait()
        for i in range(2):
            for slot in range(2):
                receive_edges(i, h, slot)

        @pl.loop(0, 2 * tile_frames)
        def _(t):
            j = lax.rem(t, tile_frames)
            slot = 1 - t // tile_frames
            below = jnp.logical_or(has_prev, j > 0)
            above = jnp.logical_or(has_next, j < tile_frames - 1)

            @pl.when(jnp.logical_and(below, above))
            def _():
                attend(h, slot, j, j, 3)

            @pl.when(jnp.logical_not(jnp.logical_and(below, above)))
            def _():
                attend(h, slot, j, jnp.where(below, j, j + 1), 2)

            @pl.when(slot == 1)
            def _():
                return_copy(h, j, row).start()

            @pl.when(slot == 0)
            def _():
                keep_copy(h, j).start()

    @pl.loop(0, half)
    def _(h):
        for i in range(3):
            row_copy(i, h).wait_send()
        for i in range(2):
            for slot in range(2):
                finish_edges(i, h, slot)
        for j in range(tile_frames):
            keep_copy(h, j).wait()
            return_copy(h, j, row).wait_send()

    @pl.loop(0, half)
    def _(h):
        for j in range(tile_frames):
            return_copy(h, j, other).wait_recv()


def pair_attention(query, keys, values):
    tile_frames, tile_size, features = query.shape
    half = features // HD // 2
    kernel = functools.partial(
        pair_kernel,
        half=half,
        tile_frames=tile_frames,
        exponent_scale=math.log2(math.e) / math.sqrt(HD),
    )
    window = (half, tile_frames + 2, 2, tile_size, HD)
    own = (half, tile_frames, 2, tile_size, HD)
    dma = pltpu.SemaphoreType.DMA
    return pl.pallas_call(
        kernel,
        out_shape=jax.ShapeDtypeStruct(query.shape, query.dtype),
        in_specs=[pl.BlockSpec(memory_space=pltpu.HBM)] * 3,
        out_specs=pl.BlockSpec(memory_space=pltpu.VMEM),
        scratch_shapes=[
            pltpu.VMEM(own, query.dtype),
            pltpu.VMEM(window, keys.dtype),
            pltpu.VMEM(window, values.dtype),
            pltpu.VMEM(own, query.dtype),
            dma((3, half)),
            dma((3, half)),
            dma((3, half)),
            dma((2, 2, 2, half)),
            dma((2, 2, 2, half)),
            dma((half, tile_frames)),
            dma((half, tile_frames)),
            dma((half, tile_frames)),
        ],
        compiler_params=pltpu.CompilerParams(
            collective_id=0, has_side_effects=True, vmem_limit_bytes=40 * 1024 * 1024
        ),
    )(*(pltpu.with_memory_space_constraint(x, pltpu.HBM) for x in (query, keys, values)))


def shift(cells, axis, forward):
    count = lax.axis_size(axis)
    if forward:
        pairs = [(i, i + 1) for i in range(count - 1)]
    else:
        pairs = [(i + 1, i) for i in range(count - 1)]
    return lax.ppermute(cells, axis, pairs)


def attention_kernel(bias_ref, q_ref, k_ref, v_ref, o_ref, *, tile_frames, score_scale):
    for j in range(tile_frames):
        q = q_ref[j]
        k = k_ref[:, j : j + 3].reshape(-1, HD)
        v = v_ref[:, j : j + 3].reshape(-1, HD)
        s = lax.dot_general(q, k, (((1,), (1,)), ((), ())), preferred_element_type=jnp.float32)
        s = s * score_scale + bias_ref[j]
        m = jnp.max(s, axis=1, keepdims=True)
        p = jnp.exp(s - m)
        l = jnp.sum(p, axis=1, keepdims=True)
        o = jnp.dot(p.astype(jnp.bfloat16), v, preferred_element_type=jnp.float32)
        o_ref[j] = (o / l).astype(o_ref.dtype)


def per_device(query, keys, values):
    frames, rows, columns, features = query.shape
    tile_frames = frames // TF
    tile_size = TF * TR * TC
    heads_here = features // HD
    score_scale = 1.0 / math.sqrt(HD)

    def tiles(x):
        return x.reshape(tile_frames, tile_size, features)

    paired = lax.axis_size("row") == 2 and lax.axis_size("frame") > 1
    if paired and heads_here % 2 == 0 and tile_frames > 1:
        out = pair_attention(tiles(query), tiles(keys), tiles(values))
        return out.reshape(query.shape)

    kv = (tiles(keys), tiles(values))
    above = shift(kv, "row", True)
    below = shift(kv, "row", False)
    own_prev = shift(tuple(x[tile_frames - 1] for x in kv), "frame", True)
    own_next = shift(tuple(x[0] for x in kv), "frame", False)
    diag_prev = shift(
        tuple(jnp.stack((a[tile_frames - 1], b[tile_frames - 1])) for a, b in zip(above, below)),
        "frame",
        True,
    )
    diag_next = shift(tuple(jnp.stack((a[0], b[0])) for a, b in zip(above, below)), "frame", False)

    def window(i):
        middle = jnp.concatenate((own_prev[i][None], kv[i], own_next[i][None]), 0)
        top = jnp.concatenate((diag_prev[i][0][None], above[i], diag_next[i][0][None]), 0)
        bottom = jnp.concatenate((diag_prev[i][1][None], below[i], diag_next[i][1][None]), 0)
        return jnp.stack((top, middle, bottom))

    key_window = window(0)
    value_window = window(1)

    frame_index = lax.axis_index("frame")
    row_index = lax.axis_index("row")
    offsets = jnp.arange(3, dtype=jnp.int32) - 1
    global_frames = frame_index * tile_frames + jnp.arange(tile_frames + 2, dtype=jnp.int32) - 1
    frame_ok = (global_frames >= 0) & (global_frames < tile_frames * lax.axis_size("frame"))
    row_ids = row_index + offsets
    row_ok = (row_ids >= 0) & (row_ids < lax.axis_size("row"))
    bias_rows = []
    for j in range(tile_frames):
        ok = row_ok[:, None] & frame_ok[None, j : j + 3]
        ok = jnp.broadcast_to(ok[:, :, None], (3, 3, tile_size)).reshape(1, 9 * tile_size)
        bias_rows.append(jnp.where(ok, 0.0, -jnp.inf).astype(jnp.float32))
    bias = jnp.stack(bias_rows)

    q = tiles(query)
    kernel = functools.partial(
        attention_kernel, tile_frames=tile_frames, score_scale=score_scale
    )
    window_block = (3, tile_frames + 2, tile_size, HD)
    out = pl.pallas_call(
        kernel,
        grid=(heads_here,),
        in_specs=[
            pl.BlockSpec((tile_frames, 1, 9 * tile_size), lambda h: (0, 0, 0)),
            pl.BlockSpec((tile_frames, tile_size, HD), lambda h: (0, 0, h)),
            pl.BlockSpec(window_block, lambda h: (0, 0, 0, h)),
            pl.BlockSpec(window_block, lambda h: (0, 0, 0, h)),
        ],
        out_specs=pl.BlockSpec((tile_frames, tile_size, HD), lambda h: (0, 0, h)),
        out_shape=jax.ShapeDtypeStruct(q.shape, query.dtype),
        compiler_params=pltpu.CompilerParams(vmem_limit_bytes=48 * 1024 * 1024),
    )(bias, q, key_window, value_window)
    return out.reshape(frames, rows, columns, features)


def solution(mesh):
    return jax.shard_map(
        per_device,
        mesh=mesh,
        in_specs=(
            P(("clips", "frame"), "row", None, "head"),
            P(("clips", "frame"), "row", None, "head"),
            P(("clips", "frame"), "row", None, "head"),
        ),
        out_specs=P(("clips", "frame"), "row", None, "head"),
        check_vma=False,
    )
```

```python
import functools
import math

import jax
import jax.numpy as jnp
from jax import lax
from jax.experimental import pallas as pl
from jax.experimental.pallas import tpu as pltpu
from jax.sharding import PartitionSpec as P

HD = 128
TF = 4
TR = 8
TC = 8
MESH = pl.DeviceIdType.MESH


def pair_kernel(
    q_ref,
    k_ref,
    v_ref,
    o_ref,
    qbuf,
    kbuf,
    vbuf,
    obuf,
    local_sem,
    x_send,
    x_recv,
    z_send,
    z_recv,
    o_send,
    o_recv,
    o_local,
    entered,
    *,
    half,
    tile_frames,
    exponent_scale,
):
    row = lax.axis_index("row")
    frame = lax.axis_index("frame")
    last_frame = lax.axis_size("frame") - 1
    other = 1 - row
    has_prev = frame > 0
    has_next = frame < last_frame

    def columns(side, h):
        return pl.ds(pl.multiple_of((side * half + h) * HD, HD), HD)

    sources = (k_ref, v_ref, q_ref)

    def place(i, h, slot):
        if i == 2:
            return qbuf.at[h, :, slot]
        return (kbuf, vbuf)[i].at[h, 1 : 1 + tile_frames, slot]

    def local_copy(i, h):
        return pltpu.make_async_copy(
            sources[i].at[:, :, columns(row, h)], place(i, h, 0), local_sem.at[i, h]
        )

    def row_copy(i, h):
        return pltpu.make_async_remote_copy(
            sources[i].at[:, :, columns(other, h)],
            place(i, h, 1),
            x_send.at[i, h],
            x_recv.at[i, h],
            device_id={"row": other},
            device_id_type=MESH,
        )

    def frame_copy(i, h, slot, up):
        buf = (kbuf, vbuf)[i]
        edge = tile_frames - 1 if up else 0
        if slot == 0:
            source = sources[i].at[edge, :, columns(row, h)]
        else:
            source = buf.at[h, 1 + edge, 1]
        return pltpu.make_async_remote_copy(
            source,
            buf.at[h, 0 if up else tile_frames + 1, slot],
            z_send.at[slot, i, int(up), h],
            z_recv.at[slot, i, int(up), h],
            device_id={"frame": frame + 1 if up else frame - 1},
            device_id_type=MESH,
        )

    def send_edges(i, h, slot):
        @pl.when(has_next)
        def _():
            frame_copy(i, h, slot, True).start()

        @pl.when(has_prev)
        def _():
            frame_copy(i, h, slot, False).start()

    def receive_edges(i, h, slot):
        @pl.when(has_prev)
        def _():
            frame_copy(i, h, slot, True).wait_recv()

        @pl.when(has_next)
        def _():
            frame_copy(i, h, slot, False).wait_recv()

    def finish_edges(i, h, slot):
        @pl.when(has_next)
        def _():
            frame_copy(i, h, slot, True).wait_send()

        @pl.when(has_prev)
        def _():
            frame_copy(i, h, slot, False).wait_send()

    def return_copy(h, j, side):
        return pltpu.make_async_remote_copy(
            obuf.at[h, j, 1],
            o_ref.at[j, :, columns(side, h)],
            o_send.at[h, j],
            o_recv.at[h, j],
            device_id={"row": other},
            device_id_type=MESH,
        )

    def keep_copy(h, j):
        return pltpu.make_async_copy(
            obuf.at[h, j, 0], o_ref.at[j, :, columns(row, h)], o_local.at[h, j]
        )

    even = lax.rem(frame, 2) == 0
    odd = jnp.logical_not(even)
    beside = has_prev.astype(jnp.int32) + has_next.astype(jnp.int32)
    barrier = pltpu.get_barrier_semaphore()

    def greet(sem, when):
        @pl.when(jnp.logical_and(when, has_next))
        def _():
            pl.semaphore_signal(sem, inc=1, device_id={"frame": frame + 1}, device_id_type=MESH)

        @pl.when(jnp.logical_and(when, has_prev))
        def _():
            pl.semaphore_signal(sem, inc=1, device_id={"frame": frame - 1}, device_id_type=MESH)

    pl.semaphore_signal(barrier, inc=1, device_id={"row": other}, device_id_type=MESH)
    greet(barrier, even)
    pl.semaphore_wait(barrier, jnp.where(odd, 1 + beside, 1))

    @pl.loop(0, half)
    def _(h):
        for i in range(3):
            row_copy(i, h).start()

    greet(entered, odd)

    @pl.loop(0, half)
    def _(h):
        for i in range(3):
            local_copy(i, h).start()

    @pl.when(even)
    def _():
        pl.semaphore_wait(entered, beside)

    @pl.loop(0, half)
    def _(h):
        for i in range(2):
            send_edges(i, h, 0)

    def attend(h, slot, j, first, count):
        q = qbuf[h, j, slot]
        k = kbuf[h, pl.ds(first, count)].reshape(-1, HD)
        v = vbuf[h, pl.ds(first, count)].reshape(-1, HD)
        s = lax.dot_general(q, k, (((1,), (1,)), ((), ())), preferred_element_type=jnp.float32)
        m = jnp.max(s, axis=1, keepdims=True)
        p = jnp.exp2((s - m) * exponent_scale)
        l = jnp.sum(p, axis=1, keepdims=True)
        o = jnp.dot(p.astype(jnp.bfloat16), v, preferred_element_type=jnp.float32)
        obuf[h, j, slot] = (o / l).astype(obuf.dtype)

    @pl.loop(0, half)
    def _(h):
        for i in range(2):
            row_copy(i, h).wait_recv()
            send_edges(i, h, 1)
        row_copy(2, h).wait_recv()
        for i in range(3):
            local_copy(i, h).wait()
        for i in range(2):
            for slot in range(2):
                receive_edges(i, h, slot)

        @pl.loop(0, 2 * tile_frames)
        def _(t):
            j = lax.rem(t, tile_frames)
            slot = 1 - t // tile_frames
            below = jnp.logical_or(has_prev, j > 0)
            above = jnp.logical_or(has_next, j < tile_frames - 1)

            @pl.when(jnp.logical_and(below, above))
            def _():
                attend(h, slot, j, j, 3)

            @pl.when(jnp.logical_not(jnp.logical_and(below, above)))
            def _():
                attend(h, slot, j, jnp.where(below, j, j + 1), 2)

            @pl.when(slot == 1)
            def _():
                return_copy(h, j, row).start()

            @pl.when(slot == 0)
            def _():
                keep_copy(h, j).start()

    @pl.loop(0, half)
    def _(h):
        for i in range(3):
            row_copy(i, h).wait_send()
        for i in range(2):
            for slot in range(2):
                finish_edges(i, h, slot)
        for j in range(tile_frames):
            keep_copy(h, j).wait()
            return_copy(h, j, row).wait_send()

    @pl.loop(0, half)
    def _(h):
        for j in range(tile_frames):
            return_copy(h, j, other).wait_recv()


def pair_attention(query, keys, values):
    tile_frames, tile_size, features = query.shape
    half = features // HD // 2
    kernel = functools.partial(
        pair_kernel,
        half=half,
        tile_frames=tile_frames,
        exponent_scale=math.log2(math.e) / math.sqrt(HD),
    )
    window = (half, tile_frames + 2, 2, tile_size, HD)
    own = (half, tile_frames, 2, tile_size, HD)
    dma = pltpu.SemaphoreType.DMA
    return pl.pallas_call(
        kernel,
        out_shape=jax.ShapeDtypeStruct(query.shape, query.dtype),
        in_specs=[pl.BlockSpec(memory_space=pltpu.HBM)] * 3,
        out_specs=pl.BlockSpec(memory_space=pltpu.VMEM),
        scratch_shapes=[
            pltpu.VMEM(own, query.dtype),
            pltpu.VMEM(window, keys.dtype),
            pltpu.VMEM(window, values.dtype),
            pltpu.VMEM(own, query.dtype),
            dma((3, half)),
            dma((3, half)),
            dma((3, half)),
            dma((2, 2, 2, half)),
            dma((2, 2, 2, half)),
            dma((half, tile_frames)),
            dma((half, tile_frames)),
            dma((half, tile_frames)),
            pltpu.SemaphoreType.REGULAR,
        ],
        compiler_params=pltpu.CompilerParams(
            collective_id=0, has_side_effects=True, vmem_limit_bytes=40 * 1024 * 1024
        ),
    )(*(pltpu.with_memory_space_constraint(x, pltpu.HBM) for x in (query, keys, values)))


def shift(cells, axis, forward):
    count = lax.axis_size(axis)
    if forward:
        pairs = [(i, i + 1) for i in range(count - 1)]
    else:
        pairs = [(i + 1, i) for i in range(count - 1)]
    return lax.ppermute(cells, axis, pairs)


def attention_kernel(bias_ref, q_ref, k_ref, v_ref, o_ref, *, tile_frames, score_scale):
    for j in range(tile_frames):
        q = q_ref[j]
        k = k_ref[:, j : j + 3].reshape(-1, HD)
        v = v_ref[:, j : j + 3].reshape(-1, HD)
        s = lax.dot_general(q, k, (((1,), (1,)), ((), ())), preferred_element_type=jnp.float32)
        s = s * score_scale + bias_ref[j]
        m = jnp.max(s, axis=1, keepdims=True)
        p = jnp.exp(s - m)
        l = jnp.sum(p, axis=1, keepdims=True)
        o = jnp.dot(p.astype(jnp.bfloat16), v, preferred_element_type=jnp.float32)
        o_ref[j] = (o / l).astype(o_ref.dtype)


def per_device(query, keys, values):
    frames, rows, columns, features = query.shape
    tile_frames = frames // TF
    tile_size = TF * TR * TC
    heads_here = features // HD
    score_scale = 1.0 / math.sqrt(HD)

    def tiles(x):
        return x.reshape(tile_frames, tile_size, features)

    paired = lax.axis_size("row") == 2 and lax.axis_size("frame") > 1
    if paired and heads_here % 2 == 0 and tile_frames > 1:
        out = pair_attention(tiles(query), tiles(keys), tiles(values))
        return out.reshape(query.shape)

    kv = (tiles(keys), tiles(values))
    above = shift(kv, "row", True)
    below = shift(kv, "row", False)
    own_prev = shift(tuple(x[tile_frames - 1] for x in kv), "frame", True)
    own_next = shift(tuple(x[0] for x in kv), "frame", False)
    diag_prev = shift(
        tuple(jnp.stack((a[tile_frames - 1], b[tile_frames - 1])) for a, b in zip(above, below)),
        "frame",
        True,
    )
    diag_next = shift(tuple(jnp.stack((a[0], b[0])) for a, b in zip(above, below)), "frame", False)

    def window(i):
        middle = jnp.concatenate((own_prev[i][None], kv[i], own_next[i][None]), 0)
        top = jnp.concatenate((diag_prev[i][0][None], above[i], diag_next[i][0][None]), 0)
        bottom = jnp.concatenate((diag_prev[i][1][None], below[i], diag_next[i][1][None]), 0)
        return jnp.stack((top, middle, bottom))

    key_window = window(0)
    value_window = window(1)

    frame_index = lax.axis_index("frame")
    row_index = lax.axis_index("row")
    offsets = jnp.arange(3, dtype=jnp.int32) - 1
    global_frames = frame_index * tile_frames + jnp.arange(tile_frames + 2, dtype=jnp.int32) - 1
    frame_ok = (global_frames >= 0) & (global_frames < tile_frames * lax.axis_size("frame"))
    row_ids = row_index + offsets
    row_ok = (row_ids >= 0) & (row_ids < lax.axis_size("row"))
    bias_rows = []
    for j in range(tile_frames):
        ok = row_ok[:, None] & frame_ok[None, j : j + 3]
        ok = jnp.broadcast_to(ok[:, :, None], (3, 3, tile_size)).reshape(1, 9 * tile_size)
        bias_rows.append(jnp.where(ok, 0.0, -jnp.inf).astype(jnp.float32))
    bias = jnp.stack(bias_rows)

    q = tiles(query)
    kernel = functools.partial(
        attention_kernel, tile_frames=tile_frames, score_scale=score_scale
    )
    window_block = (3, tile_frames + 2, tile_size, HD)
    out = pl.pallas_call(
        kernel,
        grid=(heads_here,),
        in_specs=[
            pl.BlockSpec((tile_frames, 1, 9 * tile_size), lambda h: (0, 0, 0)),
            pl.BlockSpec((tile_frames, tile_size, HD), lambda h: (0, 0, h)),
            pl.BlockSpec(window_block, lambda h: (0, 0, 0, h)),
            pl.BlockSpec(window_block, lambda h: (0, 0, 0, h)),
        ],
        out_specs=pl.BlockSpec((tile_frames, tile_size, HD), lambda h: (0, 0, h)),
        out_shape=jax.ShapeDtypeStruct(q.shape, query.dtype),
        compiler_params=pltpu.CompilerParams(vmem_limit_bytes=48 * 1024 * 1024),
    )(bias, q, key_window, value_window)
    return out.reshape(frames, rows, columns, features)


def solution(mesh):
    return jax.shard_map(
        per_device,
        mesh=mesh,
        in_specs=(
            P(("clips", "frame"), "row", None, "head"),
            P(("clips", "frame"), "row", None, "head"),
            P(("clips", "frame"), "row", None, "head"),
        ),
        out_specs=P(("clips", "frame"), "row", None, "head"),
        check_vma=False,
    )
```

```python
import functools
import math

import jax
import jax.numpy as jnp
from jax import lax
from jax.experimental import pallas as pl
from jax.experimental.pallas import tpu as pltpu
from jax.sharding import PartitionSpec as P

HD = 128
TF = 4
TR = 8
TC = 8
MESH = pl.DeviceIdType.MESH


def pair_kernel(
    q_ref,
    k_ref,
    v_ref,
    o_ref,
    qbuf,
    kbuf,
    vbuf,
    obuf,
    local_sem,
    x_send,
    x_recv,
    z_send,
    z_recv,
    f_recv,
    o_send,
    o_recv,
    o_local,
    entered,
    *,
    half,
    tile_frames,
    exponent_scale,
):
    row = lax.axis_index("row")
    frame = lax.axis_index("frame")
    last_frame = lax.axis_size("frame") - 1
    other = 1 - row
    has_prev = frame > 0
    has_next = frame < last_frame
    sources = (k_ref, v_ref, q_ref)


    def columns(side, h):
        return pl.ds(pl.multiple_of((side * half + h) * HD, HD), HD)

    def place(i, h, slot):
        if i == 2:
            return qbuf.at[h, :, slot]
        return (kbuf, vbuf)[i].at[h, 1 : 1 + tile_frames, slot]

    def local_copy(i, h):
        return pltpu.make_async_copy(
            sources[i].at[:, :, columns(row, h)], place(i, h, 0), local_sem.at[i // 2]
        )

    def across(source, target, send_sem, recv_sem):
        return pltpu.make_async_remote_copy(
            source, target, send_sem, recv_sem, device_id={"row": other}, device_id_type=MESH
        )

    def along(source, target, send_sem, recv_sem, up):
        device = {"frame": frame + 1 if up else frame - 1}
        return pltpu.make_async_remote_copy(
            source, target, send_sem, recv_sem, device_id=device, device_id_type=MESH
        )

    def row_copy(i, h):
        kind = i // 2
        source = sources[i].at[:, :, columns(other, h)]
        return across(source, place(i, h, 1), x_send.at[kind], x_recv.at[kind, h])

    def row_bytes(kind, h):
        whole = qbuf.at[h, :, 1] if kind else kbuf.at[h, 0:tile_frames]
        return across(whole, whole, x_send.at[kind], x_recv.at[kind, h])

    def send_edges(h, slot):
        for up in (True, False):

            @pl.when(has_next if up else has_prev)
            def _():
                for i in range(2):
                    buf = (kbuf, vbuf)[i]
                    edge = tile_frames - 1 if up else 0
                    target = buf.at[h, 0 if up else tile_frames + 1, slot]
                    if slot == 0:
                        source, recv = sources[i].at[edge, :, columns(row, h)], z_recv.at[int(up)]
                    else:
                        source, recv = buf.at[h, 1 + edge, 1], f_recv.at[int(up), h]
                    along(source, target, z_send.at[int(up)], recv, up).start()

    def receive_edges(h, slot):
        for up in (True, False):

            @pl.when(has_prev if up else has_next)
            def _():
                whole = kbuf.at[:, 0] if slot == 0 else kbuf.at[h, 0]
                recv = z_recv.at[int(up)] if slot == 0 else f_recv.at[int(up), h]
                along(whole, whole, z_send.at[int(up)], recv, up).wait_recv()

    def finish_edges():
        for up in (True, False):

            @pl.when(has_next if up else has_prev)
            def _():
                whole = kbuf.at[:, 0:2]
                along(whole, whole, z_send.at[int(up)], z_recv.at[int(up)], up).wait_send()

    def return_copy(h, j):
        return across(obuf.at[h, j, 1], o_ref.at[j, :, columns(row, h)], o_send, o_recv)

    def keep_copy(h, j):
        return pltpu.make_async_copy(
            obuf.at[h, j, 0], o_ref.at[j, :, columns(row, h)], o_local
        )

    even = lax.rem(frame, 2) == 0
    odd = jnp.logical_not(even)
    beside = has_prev.astype(jnp.int32) + has_next.astype(jnp.int32)
    barrier = pltpu.get_barrier_semaphore()

    def greet(sem, when):
        @pl.when(jnp.logical_and(when, has_next))
        def _():
            pl.semaphore_signal(sem, inc=1, device_id={"frame": frame + 1}, device_id_type=MESH)

        @pl.when(jnp.logical_and(when, has_prev))
        def _():
            pl.semaphore_signal(sem, inc=1, device_id={"frame": frame - 1}, device_id_type=MESH)

    pl.semaphore_signal(barrier, inc=1, device_id={"row": other}, device_id_type=MESH)
    greet(barrier, even)
    pl.semaphore_wait(barrier, jnp.where(odd, 1 + beside, 1))

    @pl.loop(0, half)
    def _(h):
        for i in range(3):
            row_copy(i, h).start()

    greet(entered, odd)

    @pl.when(even)
    def _():
        pl.semaphore_wait(entered, beside)

    @pl.loop(0, half)
    def _(h):
        send_edges(h, 0)
        for i in range(3):
            local_copy(i, h).start()

    def attend(h, slot, j, first, count):
        q = qbuf[h, j, slot]
        k = kbuf[h, pl.ds(first, count)].reshape(-1, HD)
        v = vbuf[h, pl.ds(first, count)].reshape(-1, HD)
        s = lax.dot_general(q, k, (((1,), (1,)), ((), ())), preferred_element_type=jnp.float32)
        m = jnp.max(s, axis=1, keepdims=True)
        p = jnp.exp2((s - m) * exponent_scale)
        l = jnp.sum(p, axis=1, keepdims=True)
        o = jnp.dot(p.astype(jnp.bfloat16), v, preferred_element_type=jnp.float32)
        obuf[h, j, slot] = (o / l).astype(obuf.dtype)

    @pl.loop(0, half)
    def _(h):
        row_bytes(0, h).wait_recv()
        send_edges(h, 1)
        row_bytes(1, h).wait_recv()

        @pl.when(h == 0)
        def _():
            own_kv, own_q = kbuf.at[:, 0:tile_frames], qbuf.at[:, :, 0]
            pltpu.make_async_copy(own_kv, own_kv, local_sem.at[0]).wait()
            pltpu.make_async_copy(own_q, own_q, local_sem.at[1]).wait()
            receive_edges(h, 0)

        receive_edges(h, 1)

        @pl.loop(0, 2 * tile_frames)
        def _(t):
            j = lax.rem(t, tile_frames)
            slot = 1 - t // tile_frames
            below = jnp.logical_or(has_prev, j > 0)
            above = jnp.logical_or(has_next, j < tile_frames - 1)

            @pl.when(jnp.logical_and(below, above))
            def _():
                attend(h, slot, j, j, 3)

            @pl.when(jnp.logical_not(jnp.logical_and(below, above)))
            def _():
                attend(h, slot, j, jnp.where(below, j, j + 1), 2)

            @pl.when(slot == 1)
            def _():
                return_copy(h, j).start()

            @pl.when(slot == 0)
            def _():
                keep_copy(h, j).start()

    sent_kv, sent_q, returned = kbuf.at[:, 0:tile_frames], qbuf.at[:, :, 1], obuf.at[:, :, 1]
    across(sent_kv, sent_kv, x_send.at[0], x_recv.at[0, 0]).wait_send()
    across(sent_q, sent_q, x_send.at[1], x_recv.at[1, 0]).wait_send()
    finish_edges()
    pltpu.make_async_copy(returned, returned, o_local).wait()
    across(returned, returned, o_send, o_recv).wait_send()
    across(returned, returned, o_send, o_recv).wait_recv()


def pair_attention(query, keys, values):
    tile_frames, tile_size, features = query.shape
    half = features // HD // 2
    kernel = functools.partial(
        pair_kernel,
        half=half,
        tile_frames=tile_frames,
        exponent_scale=math.log2(math.e) / math.sqrt(HD),
    )
    window = (half, tile_frames + 2, 2, tile_size, HD)
    own = (half, tile_frames, 2, tile_size, HD)
    dma = pltpu.SemaphoreType.DMA
    return pl.pallas_call(
        kernel,
        out_shape=jax.ShapeDtypeStruct(query.shape, query.dtype),
        in_specs=[pl.BlockSpec(memory_space=pltpu.HBM)] * 3,
        out_specs=pl.BlockSpec(memory_space=pltpu.VMEM),
        scratch_shapes=[
            pltpu.VMEM(own, query.dtype),
            pltpu.VMEM(window, keys.dtype),
            pltpu.VMEM(window, values.dtype),
            pltpu.VMEM(own, query.dtype),
            dma((2,)),
            dma((2,)),
            dma((2, half)),
            dma((2,)),
            dma((2,)),
            dma((2, half)),
            dma,
            dma,
            dma,
            pltpu.SemaphoreType.REGULAR,
        ],
        compiler_params=pltpu.CompilerParams(
            collective_id=0, has_side_effects=True, vmem_limit_bytes=40 * 1024 * 1024
        ),
    )(*(pltpu.with_memory_space_constraint(x, pltpu.HBM) for x in (query, keys, values)))


def shift(cells, axis, forward):
    count = lax.axis_size(axis)
    if forward:
        pairs = [(i, i + 1) for i in range(count - 1)]
    else:
        pairs = [(i + 1, i) for i in range(count - 1)]
    return lax.ppermute(cells, axis, pairs)


def attention_kernel(bias_ref, q_ref, k_ref, v_ref, o_ref, *, tile_frames, score_scale):
    for j in range(tile_frames):
        q = q_ref[j]
        k = k_ref[:, j : j + 3].reshape(-1, HD)
        v = v_ref[:, j : j + 3].reshape(-1, HD)
        s = lax.dot_general(q, k, (((1,), (1,)), ((), ())), preferred_element_type=jnp.float32)
        s = s * score_scale + bias_ref[j]
        m = jnp.max(s, axis=1, keepdims=True)
        p = jnp.exp(s - m)
        l = jnp.sum(p, axis=1, keepdims=True)
        o = jnp.dot(p.astype(jnp.bfloat16), v, preferred_element_type=jnp.float32)
        o_ref[j] = (o / l).astype(o_ref.dtype)


def per_device(query, keys, values):
    frames, rows, columns, features = query.shape
    tile_frames = frames // TF
    tile_size = TF * TR * TC
    heads_here = features // HD
    score_scale = 1.0 / math.sqrt(HD)

    def tiles(x):
        return x.reshape(tile_frames, tile_size, features)

    paired = lax.axis_size("row") == 2 and lax.axis_size("frame") > 1
    if paired and heads_here % 2 == 0 and tile_frames > 1:
        out = pair_attention(tiles(query), tiles(keys), tiles(values))
        return out.reshape(query.shape)

    kv = (tiles(keys), tiles(values))
    above = shift(kv, "row", True)
    below = shift(kv, "row", False)
    own_prev = shift(tuple(x[tile_frames - 1] for x in kv), "frame", True)
    own_next = shift(tuple(x[0] for x in kv), "frame", False)
    diag_prev = shift(
        tuple(jnp.stack((a[tile_frames - 1], b[tile_frames - 1])) for a, b in zip(above, below)),
        "frame",
        True,
    )
    diag_next = shift(tuple(jnp.stack((a[0], b[0])) for a, b in zip(above, below)), "frame", False)

    def window(i):
        middle = jnp.concatenate((own_prev[i][None], kv[i], own_next[i][None]), 0)
        top = jnp.concatenate((diag_prev[i][0][None], above[i], diag_next[i][0][None]), 0)
        bottom = jnp.concatenate((diag_prev[i][1][None], below[i], diag_next[i][1][None]), 0)
        return jnp.stack((top, middle, bottom))

    key_window = window(0)
    value_window = window(1)

    frame_index = lax.axis_index("frame")
    row_index = lax.axis_index("row")
    offsets = jnp.arange(3, dtype=jnp.int32) - 1
    global_frames = frame_index * tile_frames + jnp.arange(tile_frames + 2, dtype=jnp.int32) - 1
    frame_ok = (global_frames >= 0) & (global_frames < tile_frames * lax.axis_size("frame"))
    row_ids = row_index + offsets
    row_ok = (row_ids >= 0) & (row_ids < lax.axis_size("row"))
    bias_rows = []
    for j in range(tile_frames):
        ok = row_ok[:, None] & frame_ok[None, j : j + 3]
        ok = jnp.broadcast_to(ok[:, :, None], (3, 3, tile_size)).reshape(1, 9 * tile_size)
        bias_rows.append(jnp.where(ok, 0.0, -jnp.inf).astype(jnp.float32))
    bias = jnp.stack(bias_rows)

    q = tiles(query)
    kernel = functools.partial(
        attention_kernel, tile_frames=tile_frames, score_scale=score_scale
    )
    window_block = (3, tile_frames + 2, tile_size, HD)
    out = pl.pallas_call(
        kernel,
        grid=(heads_here,),
        in_specs=[
            pl.BlockSpec((tile_frames, 1, 9 * tile_size), lambda h: (0, 0, 0)),
            pl.BlockSpec((tile_frames, tile_size, HD), lambda h: (0, 0, h)),
            pl.BlockSpec(window_block, lambda h: (0, 0, 0, h)),
            pl.BlockSpec(window_block, lambda h: (0, 0, 0, h)),
        ],
        out_specs=pl.BlockSpec((tile_frames, tile_size, HD), lambda h: (0, 0, h)),
        out_shape=jax.ShapeDtypeStruct(q.shape, query.dtype),
        compiler_params=pltpu.CompilerParams(vmem_limit_bytes=48 * 1024 * 1024),
    )(bias, q, key_window, value_window)
    return out.reshape(frames, rows, columns, features)


def solution(mesh):
    return jax.shard_map(
        per_device,
        mesh=mesh,
        in_specs=(
            P(("clips", "frame"), "row", None, "head"),
            P(("clips", "frame"), "row", None, "head"),
            P(("clips", "frame"), "row", None, "head"),
        ),
        out_specs=P(("clips", "frame"), "row", None, "head"),
        check_vma=False,
    )
```

```python
import functools
import math

import jax
import jax.numpy as jnp
from jax import lax
from jax.experimental import pallas as pl
from jax.experimental.pallas import tpu as pltpu
from jax.sharding import PartitionSpec as P

HD = 128
TF = 4
TR = 8
TC = 8
MESH = pl.DeviceIdType.MESH


def pair_kernel(
    q_ref,
    k_ref,
    v_ref,
    o_ref,
    qbuf,
    kbuf,
    vbuf,
    obuf,
    local_sem,
    x_send,
    x_recv,
    z_send,
    z_recv,
    f_recv,
    o_send,
    o_recv,
    o_local,
    entered,
    *,
    half,
    tile_frames,
    exponent_scale,
):
    row = lax.axis_index("row")
    frame = lax.axis_index("frame")
    last_frame = lax.axis_size("frame") - 1
    other = 1 - row
    has_prev = frame > 0
    has_next = frame < last_frame
    sources = (k_ref, v_ref, q_ref)


    def columns(side, h):
        return pl.ds(pl.multiple_of((side * half + h) * HD, HD), HD)

    def place(i, h, slot):
        if i == 2:
            return qbuf.at[h, :, slot]
        return (kbuf, vbuf)[i].at[h, 1 : 1 + tile_frames, slot]

    def local_copy(i, h):
        return pltpu.make_async_copy(
            sources[i].at[:, :, columns(row, h)], place(i, h, 0), local_sem.at[i // 2]
        )

    def across(source, target, send_sem, recv_sem):
        return pltpu.make_async_remote_copy(
            source, target, send_sem, recv_sem, device_id={"row": other}, device_id_type=MESH
        )

    def along(source, target, send_sem, recv_sem, up):
        device = {"frame": frame + 1 if up else frame - 1}
        return pltpu.make_async_remote_copy(
            source, target, send_sem, recv_sem, device_id=device, device_id_type=MESH
        )

    def row_copy(i, h):
        kind = i // 2
        source = sources[i].at[:, :, columns(other, h)]
        return across(source, place(i, h, 1), x_send.at[kind], x_recv.at[kind, h])

    def row_bytes(kind, h):
        whole = qbuf.at[h, :, 1] if kind else kbuf.at[h, 0:tile_frames]
        return across(whole, whole, x_send.at[kind], x_recv.at[kind, h])

    def send_edges(h, slot):
        for up in (True, False):

            @pl.when(has_next if up else has_prev)
            def _():
                for i in range(2):
                    buf = (kbuf, vbuf)[i]
                    edge = tile_frames - 1 if up else 0
                    target = buf.at[h, 0 if up else tile_frames + 1, slot]
                    if slot == 0:
                        source, recv = sources[i].at[edge, :, columns(row, h)], z_recv.at[int(up)]
                    else:
                        source, recv = buf.at[h, 1 + edge, 1], f_recv.at[int(up), h]
                    along(source, target, z_send.at[int(up)], recv, up).start()

    def receive_edges(h, slot):
        for up in (True, False):

            @pl.when(has_prev if up else has_next)
            def _():
                whole = kbuf.at[:, 0] if slot == 0 else kbuf.at[h, 0]
                recv = z_recv.at[int(up)] if slot == 0 else f_recv.at[int(up), h]
                along(whole, whole, z_send.at[int(up)], recv, up).wait_recv()

    def finish_edges():
        for up in (True, False):

            @pl.when(has_next if up else has_prev)
            def _():
                whole = kbuf.at[:, 0:2]
                along(whole, whole, z_send.at[int(up)], z_recv.at[int(up)], up).wait_send()

    def return_copy(h, j):
        return across(obuf.at[h, j, 1], o_ref.at[j, :, columns(row, h)], o_send, o_recv)

    def keep_copy(h, j):
        return pltpu.make_async_copy(
            obuf.at[h, j, 0], o_ref.at[j, :, columns(row, h)], o_local
        )

    even = lax.rem(frame, 2) == 0
    odd = jnp.logical_not(even)
    beside = has_prev.astype(jnp.int32) + has_next.astype(jnp.int32)
    barrier = pltpu.get_barrier_semaphore()

    def greet(sem, when):
        @pl.when(jnp.logical_and(when, has_next))
        def _():
            pl.semaphore_signal(sem, inc=1, device_id={"frame": frame + 1}, device_id_type=MESH)

        @pl.when(jnp.logical_and(when, has_prev))
        def _():
            pl.semaphore_signal(sem, inc=1, device_id={"frame": frame - 1}, device_id_type=MESH)

    pl.semaphore_signal(barrier, inc=1, device_id={"row": other}, device_id_type=MESH)
    greet(barrier, even)
    pl.semaphore_wait(barrier, jnp.where(odd, 1 + beside, 1))

    @pl.loop(0, half)
    def _(h):
        for i in range(2):
            row_copy(i, h).start()

    @pl.loop(0, half)
    def _(h):
        row_copy(2, h).start()

    greet(entered, odd)

    @pl.when(even)
    def _():
        pl.semaphore_wait(entered, beside)

    @pl.loop(0, half)
    def _(h):
        send_edges(h, 0)
        for i in range(3):
            local_copy(i, h).start()

    def attend(h, slot, j, first, count):
        q = qbuf[h, j, slot]
        k = kbuf[h, pl.ds(first, count)].reshape(-1, HD)
        v = vbuf[h, pl.ds(first, count)].reshape(-1, HD)
        s = lax.dot_general(q, k, (((1,), (1,)), ((), ())), preferred_element_type=jnp.float32)
        m = jnp.max(s, axis=1, keepdims=True)
        p = jnp.exp2((s - m) * exponent_scale)
        l = jnp.sum(p, axis=1, keepdims=True)
        o = jnp.dot(p.astype(jnp.bfloat16), v, preferred_element_type=jnp.float32)
        obuf[h, j, slot] = (o / l).astype(obuf.dtype)

    @pl.loop(0, 2 * half)
    def _(step):
        remote = jnp.logical_and(step >= half - 1, step < 2 * half - 1)
        slot = remote.astype(jnp.int32)
        h = jnp.where(remote, step - half + 1, jnp.where(step < half, step, half - 1))

        @pl.when(step < half)
        def _():
            row_bytes(0, step).wait_recv()
            send_edges(step, 1)

        @pl.when(step == 0)
        def _():
            own_kv, own_q = kbuf.at[:, 0:tile_frames], qbuf.at[:, :, 0]
            pltpu.make_async_copy(own_kv, own_kv, local_sem.at[0]).wait()
            pltpu.make_async_copy(own_q, own_q, local_sem.at[1]).wait()
            receive_edges(0, 0)

        @pl.when(jnp.logical_or(step < half - 1, step == 2 * half - 2))
        def _():
            receive_edges(h, 1)

        @pl.when(remote)
        def _():
            row_bytes(1, h).wait_recv()

        @pl.loop(0, tile_frames)
        def _(j):
            below = jnp.logical_or(has_prev, j > 0)
            above = jnp.logical_or(has_next, j < tile_frames - 1)

            @pl.when(jnp.logical_and(below, above))
            def _():
                attend(h, slot, j, j, 3)

            @pl.when(jnp.logical_not(jnp.logical_and(below, above)))
            def _():
                attend(h, slot, j, jnp.where(below, j, j + 1), 2)

            @pl.when(slot == 1)
            def _():
                return_copy(h, j).start()

            @pl.when(slot == 0)
            def _():
                keep_copy(h, j).start()

    sent_kv, sent_q, returned = kbuf.at[:, 0:tile_frames], qbuf.at[:, :, 1], obuf.at[:, :, 1]
    across(sent_kv, sent_kv, x_send.at[0], x_recv.at[0, 0]).wait_send()
    across(sent_q, sent_q, x_send.at[1], x_recv.at[1, 0]).wait_send()
    finish_edges()
    pltpu.make_async_copy(returned, returned, o_local).wait()
    across(returned, returned, o_send, o_recv).wait_send()
    across(returned, returned, o_send, o_recv).wait_recv()


def pair_attention(query, keys, values):
    tile_frames, tile_size, features = query.shape
    half = features // HD // 2
    kernel = functools.partial(
        pair_kernel,
        half=half,
        tile_frames=tile_frames,
        exponent_scale=math.log2(math.e) / math.sqrt(HD),
    )
    window = (half, tile_frames + 2, 2, tile_size, HD)
    own = (half, tile_frames, 2, tile_size, HD)
    dma = pltpu.SemaphoreType.DMA
    return pl.pallas_call(
        kernel,
        out_shape=jax.ShapeDtypeStruct(query.shape, query.dtype),
        in_specs=[pl.BlockSpec(memory_space=pltpu.HBM)] * 3,
        out_specs=pl.BlockSpec(memory_space=pltpu.VMEM),
        scratch_shapes=[
            pltpu.VMEM(own, query.dtype),
            pltpu.VMEM(window, keys.dtype),
            pltpu.VMEM(window, values.dtype),
            pltpu.VMEM(own, query.dtype),
            dma((2,)),
            dma((2,)),
            dma((2, half)),
            dma((2,)),
            dma((2,)),
            dma((2, half)),
            dma,
            dma,
            dma,
            pltpu.SemaphoreType.REGULAR,
        ],
        compiler_params=pltpu.CompilerParams(
            collective_id=0, has_side_effects=True, vmem_limit_bytes=40 * 1024 * 1024
        ),
    )(*(pltpu.with_memory_space_constraint(x, pltpu.HBM) for x in (query, keys, values)))


def shift(cells, axis, forward):
    count = lax.axis_size(axis)
    if forward:
        pairs = [(i, i + 1) for i in range(count - 1)]
    else:
        pairs = [(i + 1, i) for i in range(count - 1)]
    return lax.ppermute(cells, axis, pairs)


def attention_kernel(bias_ref, q_ref, k_ref, v_ref, o_ref, *, tile_frames, score_scale):
    for j in range(tile_frames):
        q = q_ref[j]
        k = k_ref[:, j : j + 3].reshape(-1, HD)
        v = v_ref[:, j : j + 3].reshape(-1, HD)
        s = lax.dot_general(q, k, (((1,), (1,)), ((), ())), preferred_element_type=jnp.float32)
        s = s * score_scale + bias_ref[j]
        m = jnp.max(s, axis=1, keepdims=True)
        p = jnp.exp(s - m)
        l = jnp.sum(p, axis=1, keepdims=True)
        o = jnp.dot(p.astype(jnp.bfloat16), v, preferred_element_type=jnp.float32)
        o_ref[j] = (o / l).astype(o_ref.dtype)


def per_device(query, keys, values):
    frames, rows, columns, features = query.shape
    tile_frames = frames // TF
    tile_size = TF * TR * TC
    heads_here = features // HD
    score_scale = 1.0 / math.sqrt(HD)

    def tiles(x):
        return x.reshape(tile_frames, tile_size, features)

    paired = lax.axis_size("row") == 2 and lax.axis_size("frame") > 1
    if paired and heads_here % 2 == 0 and tile_frames > 1:
        out = pair_attention(tiles(query), tiles(keys), tiles(values))
        return out.reshape(query.shape)

    kv = (tiles(keys), tiles(values))
    above = shift(kv, "row", True)
    below = shift(kv, "row", False)
    own_prev = shift(tuple(x[tile_frames - 1] for x in kv), "frame", True)
    own_next = shift(tuple(x[0] for x in kv), "frame", False)
    diag_prev = shift(
        tuple(jnp.stack((a[tile_frames - 1], b[tile_frames - 1])) for a, b in zip(above, below)),
        "frame",
        True,
    )
    diag_next = shift(tuple(jnp.stack((a[0], b[0])) for a, b in zip(above, below)), "frame", False)

    def window(i):
        middle = jnp.concatenate((own_prev[i][None], kv[i], own_next[i][None]), 0)
        top = jnp.concatenate((diag_prev[i][0][None], above[i], diag_next[i][0][None]), 0)
        bottom = jnp.concatenate((diag_prev[i][1][None], below[i], diag_next[i][1][None]), 0)
        return jnp.stack((top, middle, bottom))

    key_window = window(0)
    value_window = window(1)

    frame_index = lax.axis_index("frame")
    row_index = lax.axis_index("row")
    offsets = jnp.arange(3, dtype=jnp.int32) - 1
    global_frames = frame_index * tile_frames + jnp.arange(tile_frames + 2, dtype=jnp.int32) - 1
    frame_ok = (global_frames >= 0) & (global_frames < tile_frames * lax.axis_size("frame"))
    row_ids = row_index + offsets
    row_ok = (row_ids >= 0) & (row_ids < lax.axis_size("row"))
    bias_rows = []
    for j in range(tile_frames):
        ok = row_ok[:, None] & frame_ok[None, j : j + 3]
        ok = jnp.broadcast_to(ok[:, :, None], (3, 3, tile_size)).reshape(1, 9 * tile_size)
        bias_rows.append(jnp.where(ok, 0.0, -jnp.inf).astype(jnp.float32))
    bias = jnp.stack(bias_rows)

    q = tiles(query)
    kernel = functools.partial(
        attention_kernel, tile_frames=tile_frames, score_scale=score_scale
    )
    window_block = (3, tile_frames + 2, tile_size, HD)
    out = pl.pallas_call(
        kernel,
        grid=(heads_here,),
        in_specs=[
            pl.BlockSpec((tile_frames, 1, 9 * tile_size), lambda h: (0, 0, 0)),
            pl.BlockSpec((tile_frames, tile_size, HD), lambda h: (0, 0, h)),
            pl.BlockSpec(window_block, lambda h: (0, 0, 0, h)),
            pl.BlockSpec(window_block, lambda h: (0, 0, 0, h)),
        ],
        out_specs=pl.BlockSpec((tile_frames, tile_size, HD), lambda h: (0, 0, h)),
        out_shape=jax.ShapeDtypeStruct(q.shape, query.dtype),
        compiler_params=pltpu.CompilerParams(vmem_limit_bytes=48 * 1024 * 1024),
    )(bias, q, key_window, value_window)
    return out.reshape(frames, rows, columns, features)


def solution(mesh):
    return jax.shard_map(
        per_device,
        mesh=mesh,
        in_specs=(
            P(("clips", "frame"), "row", None, "head"),
            P(("clips", "frame"), "row", None, "head"),
            P(("clips", "frame"), "row", None, "head"),
        ),
        out_specs=P(("clips", "frame"), "row", None, "head"),
        check_vma=False,
    )
```

```python
import functools
import math

import jax
import jax.numpy as jnp
from jax import lax
from jax.experimental import pallas as pl
from jax.experimental.pallas import tpu as pltpu
from jax.sharding import PartitionSpec as P

HD = 128
TF = 4
TR = 8
TC = 8
MESH = pl.DeviceIdType.MESH


def pair_kernel(
    q_ref,
    k_ref,
    v_ref,
    o_ref,
    held,
    obuf,
    local_sem,
    x_send,
    x_recv,
    z_send,
    z_recv,
    f_recv,
    o_recv,
    entered,
    *,
    half,
    tile_frames,
    exponent_scale,
):
    row = lax.axis_index("row")
    frame = lax.axis_index("frame")
    last_frame = lax.axis_size("frame") - 1
    other = 1 - row
    has_prev = frame > 0
    has_next = frame < last_frame
    sources = (k_ref, v_ref, q_ref)


    def columns(side, h):
        return pl.ds(pl.multiple_of((side * half + h) * HD, HD), HD)

    def place(i, h, slot):
        return held.at[i, h, 1 : 1 + tile_frames, slot]

    def local_copy(i, h):
        return pltpu.make_async_copy(
            sources[i].at[:, :, columns(row, h)], place(i, h, 0), local_sem
        )

    def across(source, target, send_sem, recv_sem):
        return pltpu.make_async_remote_copy(
            source, target, send_sem, recv_sem, device_id={"row": other}, device_id_type=MESH
        )

    def along(source, target, send_sem, recv_sem, up):
        device = {"frame": frame + 1 if up else frame - 1}
        return pltpu.make_async_remote_copy(
            source, target, send_sem, recv_sem, device_id=device, device_id_type=MESH
        )

    def row_copy(i, h):
        kind = i // 2
        source = sources[i].at[:, :, columns(other, h)]
        return across(source, place(i, h, 1), x_send, x_recv.at[kind, h])

    def row_bytes(kind, h):
        whole = held.at[2, h, 0:tile_frames, 1] if kind else held.at[0, h, 0:tile_frames]
        return across(whole, whole, x_send, x_recv.at[kind, h])

    def send_edges(h, slot):
        for up in (True, False):

            @pl.when(has_next if up else has_prev)
            def _():
                for i in range(2):
                    edge = tile_frames - 1 if up else 0
                    target = held.at[i, h, 0 if up else tile_frames + 1, slot]
                    if slot == 0:
                        source, recv = sources[i].at[edge, :, columns(row, h)], z_recv
                    else:
                        source, recv = held.at[i, h, 1 + edge, 1], f_recv.at[h]
                    along(source, target, z_send, recv, up).start()

    def by_neighbours(one, two, wait):
        both = jnp.logical_and(has_prev, has_next)

        @pl.when(both)
        def _():
            wait(two)

        @pl.when(jnp.logical_not(both))
        def _():
            wait(one)

    def receive_edges(h, slot):
        one = held.at[0, :, 0] if slot == 0 else held.at[0, h, 0]
        two = held.at[0, :, 0:2] if slot == 0 else held.at[0, h, 0:2]
        recv = z_recv if slot == 0 else f_recv.at[h]
        by_neighbours(one, two, lambda whole: across(whole, whole, z_send, recv).wait_recv())

    def finish_edges():
        one, two = held.at[0, :, 0:2], held.at[0:2, :, 0:2]
        by_neighbours(one, two, lambda whole: across(whole, whole, z_send, z_recv).wait_send())

    def return_copy(h, j):
        return across(obuf.at[h, j, 1], o_ref.at[j, :, columns(row, h)], x_send, o_recv)

    def keep_copy(h, j):
        return pltpu.make_async_copy(
            obuf.at[h, j, 0], o_ref.at[j, :, columns(row, h)], local_sem
        )

    even = lax.rem(frame, 2) == 0
    odd = jnp.logical_not(even)
    beside = has_prev.astype(jnp.int32) + has_next.astype(jnp.int32)
    barrier = pltpu.get_barrier_semaphore()

    def greet(sem, when):
        @pl.when(jnp.logical_and(when, has_next))
        def _():
            pl.semaphore_signal(sem, inc=1, device_id={"frame": frame + 1}, device_id_type=MESH)

        @pl.when(jnp.logical_and(when, has_prev))
        def _():
            pl.semaphore_signal(sem, inc=1, device_id={"frame": frame - 1}, device_id_type=MESH)

    pl.semaphore_signal(barrier, inc=1, device_id={"row": other}, device_id_type=MESH)
    greet(barrier, even)
    pl.semaphore_wait(barrier, jnp.where(odd, 1 + beside, 1))

    @pl.loop(0, half)
    def _(h):
        for i in range(2):
            row_copy(i, h).start()

    @pl.loop(0, half)
    def _(h):
        row_copy(2, h).start()

    greet(entered, odd)

    @pl.when(even)
    def _():
        pl.semaphore_wait(entered, beside)

    @pl.loop(0, half)
    def _(h):
        send_edges(h, 0)
        for i in range(3):
            local_copy(i, h).start()

    def attend(h, slot, j, first, count):
        q = held[2, h, 1 + j, slot]
        k = held[0, h, pl.ds(first, count)].reshape(-1, HD)
        v = held[1, h, pl.ds(first, count)].reshape(-1, HD)
        s = lax.dot_general(q, k, (((1,), (1,)), ((), ())), preferred_element_type=jnp.float32)
        m = jnp.max(s, axis=1, keepdims=True)
        p = jnp.exp2((s - m) * exponent_scale)
        l = jnp.sum(p, axis=1, keepdims=True)
        o = jnp.dot(p.astype(jnp.bfloat16), v, preferred_element_type=jnp.float32)
        obuf[h, j, slot] = (o / l).astype(obuf.dtype)

    @pl.loop(0, 2 * half)
    def _(step):
        remote = jnp.logical_and(step >= half - 1, step < 2 * half - 1)
        slot = remote.astype(jnp.int32)
        h = jnp.where(remote, step - half + 1, jnp.where(step < half, step, half - 1))

        @pl.when(step < half)
        def _():
            row_bytes(0, step).wait_recv()
            send_edges(step, 1)

        @pl.when(step == 0)
        def _():
            own = held.at[:, :, 1 : 1 + tile_frames, 0]
            pltpu.make_async_copy(own, own, local_sem).wait()
            receive_edges(0, 0)

        @pl.when(jnp.logical_or(step < half - 1, step == 2 * half - 2))
        def _():
            receive_edges(h, 1)

        @pl.when(remote)
        def _():
            row_bytes(1, h).wait_recv()

        @pl.loop(0, tile_frames)
        def _(j):
            below = jnp.logical_or(has_prev, j > 0)
            above = jnp.logical_or(has_next, j < tile_frames - 1)

            @pl.when(jnp.logical_and(below, above))
            def _():
                attend(h, slot, j, j, 3)

            @pl.when(jnp.logical_not(jnp.logical_and(below, above)))
            def _():
                attend(h, slot, j, jnp.where(below, j, j + 1), 2)

            @pl.when(slot == 1)
            def _():
                return_copy(h, j).start()

            @pl.when(slot == 0)
            def _():
                keep_copy(h, j).start()

    sent, returned = held.at[0:2, :, 0:tile_frames], obuf.at[:, :, 1]
    finish_edges()
    pltpu.make_async_copy(returned, returned, local_sem).wait()
    across(sent, sent, x_send, o_recv).wait_send()
    across(returned, returned, x_send, o_recv).wait_recv()


def pair_attention(query, keys, values):
    tile_frames, tile_size, features = query.shape
    half = features // HD // 2
    kernel = functools.partial(
        pair_kernel,
        half=half,
        tile_frames=tile_frames,
        exponent_scale=math.log2(math.e) / math.sqrt(HD),
    )
    window = (3, half, tile_frames + 2, 2, tile_size, HD)
    own = (half, tile_frames, 2, tile_size, HD)
    dma = pltpu.SemaphoreType.DMA
    return pl.pallas_call(
        kernel,
        out_shape=jax.ShapeDtypeStruct(query.shape, query.dtype),
        in_specs=[pl.BlockSpec(memory_space=pltpu.HBM)] * 3,
        out_specs=pl.BlockSpec(memory_space=pltpu.VMEM),
        scratch_shapes=[
            pltpu.VMEM(window, query.dtype),
            pltpu.VMEM(own, query.dtype),
            dma,
            dma,
            dma((2, half)),
            dma,
            dma,
            dma((half,)),
            dma,
            pltpu.SemaphoreType.REGULAR,
        ],
        compiler_params=pltpu.CompilerParams(
            collective_id=0, has_side_effects=True, vmem_limit_bytes=40 * 1024 * 1024
        ),
    )(*(pltpu.with_memory_space_constraint(x, pltpu.HBM) for x in (query, keys, values)))


def shift(cells, axis, forward):
    count = lax.axis_size(axis)
    if forward:
        pairs = [(i, i + 1) for i in range(count - 1)]
    else:
        pairs = [(i + 1, i) for i in range(count - 1)]
    return lax.ppermute(cells, axis, pairs)


def attention_kernel(bias_ref, q_ref, k_ref, v_ref, o_ref, *, tile_frames, score_scale):
    for j in range(tile_frames):
        q = q_ref[j]
        k = k_ref[:, j : j + 3].reshape(-1, HD)
        v = v_ref[:, j : j + 3].reshape(-1, HD)
        s = lax.dot_general(q, k, (((1,), (1,)), ((), ())), preferred_element_type=jnp.float32)
        s = s * score_scale + bias_ref[j]
        m = jnp.max(s, axis=1, keepdims=True)
        p = jnp.exp(s - m)
        l = jnp.sum(p, axis=1, keepdims=True)
        o = jnp.dot(p.astype(jnp.bfloat16), v, preferred_element_type=jnp.float32)
        o_ref[j] = (o / l).astype(o_ref.dtype)


def per_device(query, keys, values):
    frames, rows, columns, features = query.shape
    tile_frames = frames // TF
    tile_size = TF * TR * TC
    heads_here = features // HD
    score_scale = 1.0 / math.sqrt(HD)

    def tiles(x):
        return x.reshape(tile_frames, tile_size, features)

    paired = lax.axis_size("row") == 2 and lax.axis_size("frame") > 1
    if paired and heads_here % 2 == 0 and tile_frames > 1:
        out = pair_attention(tiles(query), tiles(keys), tiles(values))
        return out.reshape(query.shape)

    kv = (tiles(keys), tiles(values))
    above = shift(kv, "row", True)
    below = shift(kv, "row", False)
    own_prev = shift(tuple(x[tile_frames - 1] for x in kv), "frame", True)
    own_next = shift(tuple(x[0] for x in kv), "frame", False)
    diag_prev = shift(
        tuple(jnp.stack((a[tile_frames - 1], b[tile_frames - 1])) for a, b in zip(above, below)),
        "frame",
        True,
    )
    diag_next = shift(tuple(jnp.stack((a[0], b[0])) for a, b in zip(above, below)), "frame", False)

    def window(i):
        middle = jnp.concatenate((own_prev[i][None], kv[i], own_next[i][None]), 0)
        top = jnp.concatenate((diag_prev[i][0][None], above[i], diag_next[i][0][None]), 0)
        bottom = jnp.concatenate((diag_prev[i][1][None], below[i], diag_next[i][1][None]), 0)
        return jnp.stack((top, middle, bottom))

    key_window = window(0)
    value_window = window(1)

    frame_index = lax.axis_index("frame")
    row_index = lax.axis_index("row")
    offsets = jnp.arange(3, dtype=jnp.int32) - 1
    global_frames = frame_index * tile_frames + jnp.arange(tile_frames + 2, dtype=jnp.int32) - 1
    frame_ok = (global_frames >= 0) & (global_frames < tile_frames * lax.axis_size("frame"))
    row_ids = row_index + offsets
    row_ok = (row_ids >= 0) & (row_ids < lax.axis_size("row"))
    bias_rows = []
    for j in range(tile_frames):
        ok = row_ok[:, None] & frame_ok[None, j : j + 3]
        ok = jnp.broadcast_to(ok[:, :, None], (3, 3, tile_size)).reshape(1, 9 * tile_size)
        bias_rows.append(jnp.where(ok, 0.0, -jnp.inf).astype(jnp.float32))
    bias = jnp.stack(bias_rows)

    q = tiles(query)
    kernel = functools.partial(
        attention_kernel, tile_frames=tile_frames, score_scale=score_scale
    )
    window_block = (3, tile_frames + 2, tile_size, HD)
    out = pl.pallas_call(
        kernel,
        grid=(heads_here,),
        in_specs=[
            pl.BlockSpec((tile_frames, 1, 9 * tile_size), lambda h: (0, 0, 0)),
            pl.BlockSpec((tile_frames, tile_size, HD), lambda h: (0, 0, h)),
            pl.BlockSpec(window_block, lambda h: (0, 0, 0, h)),
            pl.BlockSpec(window_block, lambda h: (0, 0, 0, h)),
        ],
        out_specs=pl.BlockSpec((tile_frames, tile_size, HD), lambda h: (0, 0, h)),
        out_shape=jax.ShapeDtypeStruct(q.shape, query.dtype),
        compiler_params=pltpu.CompilerParams(vmem_limit_bytes=48 * 1024 * 1024),
    )(bias, q, key_window, value_window)
    return out.reshape(frames, rows, columns, features)


def solution(mesh):
    return jax.shard_map(
        per_device,
        mesh=mesh,
        in_specs=(
            P(("clips", "frame"), "row", None, "head"),
            P(("clips", "frame"), "row", None, "head"),
            P(("clips", "frame"), "row", None, "head"),
        ),
        out_specs=P(("clips", "frame"), "row", None, "head"),
        check_vma=False,
    )
```

```python
import functools
import math

import jax
import jax.numpy as jnp
from jax import lax
from jax.experimental import pallas as pl
from jax.experimental.pallas import tpu as pltpu
from jax.sharding import PartitionSpec as P

HD = 128
TF = 4
TR = 8
TC = 8
MESH = pl.DeviceIdType.MESH


def pair_kernel(
    q_ref,
    k_ref,
    v_ref,
    o_ref,
    held,
    obuf,
    local_sem,
    x_send,
    x_recv,
    z_send,
    z_recv,
    f_recv,
    o_recv,
    entered,
    *,
    half,
    tile_frames,
    exponent_scale,
):
    row = lax.axis_index("row")
    frame = lax.axis_index("frame")
    last_frame = lax.axis_size("frame") - 1
    other = 1 - row
    has_prev = frame > 0
    has_next = frame < last_frame
    sources = (k_ref, v_ref, q_ref)


    def columns(side, h):
        return pl.ds(pl.multiple_of((side * half + h) * HD, HD), HD)

    def place(i, h, slot):
        return held.at[i, h, 1 : 1 + tile_frames, slot]

    def local_copy(i, h):
        return pltpu.make_async_copy(
            sources[i].at[:, :, columns(row, h)], place(i, h, 0), local_sem
        )

    def across(source, target, send_sem, recv_sem):
        return pltpu.make_async_remote_copy(
            source, target, send_sem, recv_sem, device_id={"row": other}, device_id_type=MESH
        )

    def along(source, target, send_sem, recv_sem, up):
        device = {"frame": frame + 1 if up else frame - 1}
        return pltpu.make_async_remote_copy(
            source, target, send_sem, recv_sem, device_id=device, device_id_type=MESH
        )

    def row_copy(i, h, first=0):
        kind = i // 2
        sem = x_send.at[0 if kind else first or 2]
        source = sources[i].at[:, :, columns(other, h)]
        return across(source, place(i, h, 1), sem, x_recv.at[kind, h])

    def row_bytes(kind, h):
        whole = held.at[2, h, 0:tile_frames, 1] if kind else held.at[0, h, 0:tile_frames]
        return across(whole, whole, x_send.at[0], x_recv.at[kind, h])

    def send_edges(h, slot):
        for up in (True, False):

            @pl.when(has_next if up else has_prev)
            def _():
                for i in range(2):
                    edge = tile_frames - 1 if up else 0
                    target = held.at[i, h, 0 if up else tile_frames + 1, slot]
                    if slot == 0:
                        source, recv = sources[i].at[edge, :, columns(row, h)], z_recv
                    else:
                        source, recv = held.at[i, h, 1 + edge, 1], f_recv.at[h]
                    along(source, target, z_send, recv, up).start()

    def by_neighbours(one, two, wait):
        both = jnp.logical_and(has_prev, has_next)

        @pl.when(both)
        def _():
            wait(two)

        @pl.when(jnp.logical_not(both))
        def _():
            wait(one)

    def receive_edges(h, slot):
        one = held.at[0, :, 0] if slot == 0 else held.at[0, h, 0]
        two = held.at[0, :, 0:2] if slot == 0 else held.at[0, h, 0:2]
        recv = z_recv if slot == 0 else f_recv.at[h]
        by_neighbours(one, two, lambda whole: across(whole, whole, z_send, recv).wait_recv())

    def finish_edges():
        one, two = held.at[0, :, 0:2], held.at[0:2, :, 0:2]
        by_neighbours(one, two, lambda whole: across(whole, whole, z_send, z_recv).wait_send())

    def return_copy(h, j):
        return across(obuf.at[h, j, 1], o_ref.at[j, :, columns(row, h)], x_send.at[0], o_recv)

    def keep_copy(h, j):
        return pltpu.make_async_copy(
            obuf.at[h, j, 0], o_ref.at[j, :, columns(row, h)], local_sem
        )

    even = lax.rem(frame, 2) == 0
    odd = jnp.logical_not(even)
    beside = has_prev.astype(jnp.int32) + has_next.astype(jnp.int32)
    barrier = pltpu.get_barrier_semaphore()

    def greet(sem, when):
        @pl.when(jnp.logical_and(when, has_next))
        def _():
            pl.semaphore_signal(sem, inc=1, device_id={"frame": frame + 1}, device_id_type=MESH)

        @pl.when(jnp.logical_and(when, has_prev))
        def _():
            pl.semaphore_signal(sem, inc=1, device_id={"frame": frame - 1}, device_id_type=MESH)

    pl.semaphore_signal(barrier, inc=1, device_id={"row": other}, device_id_type=MESH)
    greet(barrier, even)
    pl.semaphore_wait(barrier, jnp.where(odd, 1 + beside, 1))

    for i in range(2):
        row_copy(i, 0, 1).start()

    greet(entered, odd)

    @pl.when(even)
    def _():
        pl.semaphore_wait(entered, beside)

    @pl.loop(0, half)
    def _(h):
        send_edges(h, 0)
        for i in range(3):
            local_copy(i, h).start()

    yields = lax.axis_index("head") == 1
    leaving = held.at[0, 0, 0:tile_frames]

    @pl.when(yields)
    def _():
        across(leaving, leaving, x_send.at[1], o_recv).wait_send()

    if half > 1:
        for i in range(2):
            row_copy(i, 1, 3).start()

        @pl.when(yields)
        def _():
            across(leaving, leaving, x_send.at[3], o_recv).wait_send()

    @pl.loop(2, half)
    def _(h):
        for i in range(2):
            row_copy(i, h).start()

    @pl.loop(0, half)
    def _(h):
        row_copy(2, h).start()

    def attend(h, slot, j, first, count):
        q = held[2, h, 1 + j, slot]
        k = held[0, h, pl.ds(first, count)].reshape(-1, HD)
        v = held[1, h, pl.ds(first, count)].reshape(-1, HD)
        s = lax.dot_general(q, k, (((1,), (1,)), ((), ())), preferred_element_type=jnp.float32)
        m = jnp.max(s, axis=1, keepdims=True)
        p = jnp.exp2((s - m) * exponent_scale)
        l = jnp.sum(p, axis=1, keepdims=True)
        o = jnp.dot(p.astype(jnp.bfloat16), v, preferred_element_type=jnp.float32)
        obuf[h, j, slot] = (o / l).astype(obuf.dtype)

    @pl.loop(0, 2 * half)
    def _(step):
        remote = jnp.logical_and(step >= half - 1, step < 2 * half - 1)
        slot = remote.astype(jnp.int32)
        h = jnp.where(remote, step - half + 1, jnp.where(step < half, step, half - 1))

        @pl.when(step < half)
        def _():
            row_bytes(0, step).wait_recv()
            send_edges(step, 1)

        @pl.when(step == 0)
        def _():
            own = held.at[:, :, 1 : 1 + tile_frames, 0]
            pltpu.make_async_copy(own, own, local_sem).wait()
            receive_edges(0, 0)

        @pl.when(jnp.logical_or(step < half - 1, step == 2 * half - 2))
        def _():
            receive_edges(h, 1)

        @pl.when(remote)
        def _():
            row_bytes(1, h).wait_recv()

        @pl.loop(0, tile_frames)
        def _(j):
            below = jnp.logical_or(has_prev, j > 0)
            above = jnp.logical_or(has_next, j < tile_frames - 1)

            @pl.when(jnp.logical_and(below, above))
            def _():
                attend(h, slot, j, j, 3)

            @pl.when(jnp.logical_not(jnp.logical_and(below, above)))
            def _():
                attend(h, slot, j, jnp.where(below, j, j + 1), 2)

            @pl.when(slot == 1)
            def _():
                return_copy(h, j).start()

            @pl.when(slot == 0)
            def _():
                keep_copy(h, j).start()

    sent, returned = held.at[0, :, 0:tile_frames], obuf.at[:, :, 1]
    finish_edges()
    pltpu.make_async_copy(returned, returned, local_sem).wait()
    across(sent, sent, x_send.at[0], o_recv).wait_send()

    @pl.when(jnp.logical_not(yields))
    def _():
        across(leaving, leaving, x_send.at[1], o_recv).wait_send()
        if half > 1:
            across(leaving, leaving, x_send.at[3], o_recv).wait_send()

    if half > 2:
        later = held.at[0, 0 : half - 2, 0:tile_frames]
        across(later, later, x_send.at[2], o_recv).wait_send()
    across(returned, returned, x_send.at[0], o_recv).wait_recv()


def pair_attention(query, keys, values):
    tile_frames, tile_size, features = query.shape
    half = features // HD // 2
    kernel = functools.partial(
        pair_kernel,
        half=half,
        tile_frames=tile_frames,
        exponent_scale=math.log2(math.e) / math.sqrt(HD),
    )
    window = (3, half, tile_frames + 2, 2, tile_size, HD)
    own = (half, tile_frames, 2, tile_size, HD)
    dma = pltpu.SemaphoreType.DMA
    return pl.pallas_call(
        kernel,
        out_shape=jax.ShapeDtypeStruct(query.shape, query.dtype),
        in_specs=[pl.BlockSpec(memory_space=pltpu.HBM)] * 3,
        out_specs=pl.BlockSpec(memory_space=pltpu.VMEM),
        scratch_shapes=[
            pltpu.VMEM(window, query.dtype),
            pltpu.VMEM(own, query.dtype),
            dma,
            dma((4,)),
            dma((2, half)),
            dma,
            dma,
            dma((half,)),
            dma,
            pltpu.SemaphoreType.REGULAR,
        ],
        compiler_params=pltpu.CompilerParams(
            collective_id=0, has_side_effects=True, vmem_limit_bytes=40 * 1024 * 1024
        ),
    )(*(pltpu.with_memory_space_constraint(x, pltpu.HBM) for x in (query, keys, values)))


def shift(cells, axis, forward):
    count = lax.axis_size(axis)
    if forward:
        pairs = [(i, i + 1) for i in range(count - 1)]
    else:
        pairs = [(i + 1, i) for i in range(count - 1)]
    return lax.ppermute(cells, axis, pairs)


def attention_kernel(bias_ref, q_ref, k_ref, v_ref, o_ref, *, tile_frames, score_scale):
    for j in range(tile_frames):
        q = q_ref[j]
        k = k_ref[:, j : j + 3].reshape(-1, HD)
        v = v_ref[:, j : j + 3].reshape(-1, HD)
        s = lax.dot_general(q, k, (((1,), (1,)), ((), ())), preferred_element_type=jnp.float32)
        s = s * score_scale + bias_ref[j]
        m = jnp.max(s, axis=1, keepdims=True)
        p = jnp.exp(s - m)
        l = jnp.sum(p, axis=1, keepdims=True)
        o = jnp.dot(p.astype(jnp.bfloat16), v, preferred_element_type=jnp.float32)
        o_ref[j] = (o / l).astype(o_ref.dtype)


def per_device(query, keys, values):
    frames, rows, columns, features = query.shape
    tile_frames = frames // TF
    tile_size = TF * TR * TC
    heads_here = features // HD
    score_scale = 1.0 / math.sqrt(HD)

    def tiles(x):
        return x.reshape(tile_frames, tile_size, features)

    paired = lax.axis_size("row") == 2 and lax.axis_size("frame") > 1
    if paired and heads_here % 2 == 0 and tile_frames > 1:
        out = pair_attention(tiles(query), tiles(keys), tiles(values))
        return out.reshape(query.shape)

    kv = (tiles(keys), tiles(values))
    above = shift(kv, "row", True)
    below = shift(kv, "row", False)
    own_prev = shift(tuple(x[tile_frames - 1] for x in kv), "frame", True)
    own_next = shift(tuple(x[0] for x in kv), "frame", False)
    diag_prev = shift(
        tuple(jnp.stack((a[tile_frames - 1], b[tile_frames - 1])) for a, b in zip(above, below)),
        "frame",
        True,
    )
    diag_next = shift(tuple(jnp.stack((a[0], b[0])) for a, b in zip(above, below)), "frame", False)

    def window(i):
        middle = jnp.concatenate((own_prev[i][None], kv[i], own_next[i][None]), 0)
        top = jnp.concatenate((diag_prev[i][0][None], above[i], diag_next[i][0][None]), 0)
        bottom = jnp.concatenate((diag_prev[i][1][None], below[i], diag_next[i][1][None]), 0)
        return jnp.stack((top, middle, bottom))

    key_window = window(0)
    value_window = window(1)

    frame_index = lax.axis_index("frame")
    row_index = lax.axis_index("row")
    offsets = jnp.arange(3, dtype=jnp.int32) - 1
    global_frames = frame_index * tile_frames + jnp.arange(tile_frames + 2, dtype=jnp.int32) - 1
    frame_ok = (global_frames >= 0) & (global_frames < tile_frames * lax.axis_size("frame"))
    row_ids = row_index + offsets
    row_ok = (row_ids >= 0) & (row_ids < lax.axis_size("row"))
    bias_rows = []
    for j in range(tile_frames):
        ok = row_ok[:, None] & frame_ok[None, j : j + 3]
        ok = jnp.broadcast_to(ok[:, :, None], (3, 3, tile_size)).reshape(1, 9 * tile_size)
        bias_rows.append(jnp.where(ok, 0.0, -jnp.inf).astype(jnp.float32))
    bias = jnp.stack(bias_rows)

    q = tiles(query)
    kernel = functools.partial(
        attention_kernel, tile_frames=tile_frames, score_scale=score_scale
    )
    window_block = (3, tile_frames + 2, tile_size, HD)
    out = pl.pallas_call(
        kernel,
        grid=(heads_here,),
        in_specs=[
            pl.BlockSpec((tile_frames, 1, 9 * tile_size), lambda h: (0, 0, 0)),
            pl.BlockSpec((tile_frames, tile_size, HD), lambda h: (0, 0, h)),
            pl.BlockSpec(window_block, lambda h: (0, 0, 0, h)),
            pl.BlockSpec(window_block, lambda h: (0, 0, 0, h)),
        ],
        out_specs=pl.BlockSpec((tile_frames, tile_size, HD), lambda h: (0, 0, h)),
        out_shape=jax.ShapeDtypeStruct(q.shape, query.dtype),
        compiler_params=pltpu.CompilerParams(vmem_limit_bytes=48 * 1024 * 1024),
    )(bias, q, key_window, value_window)
    return out.reshape(frames, rows, columns, features)


def solution(mesh):
    return jax.shard_map(
        per_device,
        mesh=mesh,
        in_specs=(
            P(("clips", "frame"), "row", None, "head"),
            P(("clips", "frame"), "row", None, "head"),
            P(("clips", "frame"), "row", None, "head"),
        ),
        out_specs=P(("clips", "frame"), "row", None, "head"),
        check_vma=False,
    )
```

```python
import functools
import math

import jax
import jax.numpy as jnp
from jax import lax
from jax.experimental import pallas as pl
from jax.experimental.pallas import tpu as pltpu
from jax.sharding import PartitionSpec as P

HD = 128
TF = 4
TR = 8
TC = 8
MESH = pl.DeviceIdType.MESH


def pair_kernel(
    q_ref,
    k_ref,
    v_ref,
    o_ref,
    held,
    obuf,
    local_sem,
    x_send,
    x_recv,
    z_send,
    z_recv,
    f_recv,
    o_recv,
    entered,
    *,
    half,
    tile_frames,
    exponent_scale,
):
    row = lax.axis_index("row")
    frame = lax.axis_index("frame")
    last_frame = lax.axis_size("frame") - 1
    other = 1 - row
    has_prev = frame > 0
    has_next = frame < last_frame
    sources = (k_ref, v_ref, q_ref)


    def columns(side, h):
        return pl.ds(pl.multiple_of((side * half + h) * HD, HD), HD)

    def place(i, h, slot):
        return held.at[i, h, 1 : 1 + tile_frames, slot]

    def local_copy(i, h):
        return pltpu.make_async_copy(
            sources[i].at[:, :, columns(row, h)], place(i, h, 0), local_sem
        )

    def across(source, target, send_sem, recv_sem):
        return pltpu.make_async_remote_copy(
            source, target, send_sem, recv_sem, device_id={"row": other}, device_id_type=MESH
        )

    def along(source, target, send_sem, recv_sem, up):
        device = {"frame": frame + 1 if up else frame - 1}
        return pltpu.make_async_remote_copy(
            source, target, send_sem, recv_sem, device_id=device, device_id_type=MESH
        )

    def row_copy(i, h):
        kind = i // 2
        source = sources[i].at[:, :, columns(other, h)]
        return across(source, place(i, h, 1), x_send.at[1 - kind], x_recv.at[kind, h])

    def row_bytes(kind, h):
        whole = held.at[2, h, 0:tile_frames, 1] if kind else held.at[0, h, 0:tile_frames]
        return across(whole, whole, x_send.at[0], x_recv.at[kind, h])

    def send_edges(h, slot):
        for up in (True, False):

            @pl.when(has_next if up else has_prev)
            def _():
                for i in range(2):
                    edge = tile_frames - 1 if up else 0
                    target = held.at[i, h, 0 if up else tile_frames + 1, slot]
                    if slot == 0:
                        source, recv = sources[i].at[edge, :, columns(row, h)], z_recv
                    else:
                        source, recv = held.at[i, h, 1 + edge, 1], f_recv.at[h]
                    along(source, target, z_send, recv, up).start()

    def by_neighbours(one, two, wait):
        both = jnp.logical_and(has_prev, has_next)

        @pl.when(both)
        def _():
            wait(two)

        @pl.when(jnp.logical_not(both))
        def _():
            wait(one)

    def receive_edges(h, slot):
        one = held.at[0, :, 0] if slot == 0 else held.at[0, h, 0]
        two = held.at[0, :, 0:2] if slot == 0 else held.at[0, h, 0:2]
        recv = z_recv if slot == 0 else f_recv.at[h]
        by_neighbours(one, two, lambda whole: across(whole, whole, z_send, recv).wait_recv())

    def finish_edges():
        one, two = held.at[0, :, 0:2], held.at[0:2, :, 0:2]
        by_neighbours(one, two, lambda whole: across(whole, whole, z_send, z_recv).wait_send())

    def return_copy(h, j):
        return across(obuf.at[h, j, 1], o_ref.at[j, :, columns(row, h)], x_send.at[0], o_recv)

    def keep_copy(h, j):
        return pltpu.make_async_copy(
            obuf.at[h, j, 0], o_ref.at[j, :, columns(row, h)], local_sem
        )

    even = lax.rem(frame, 2) == 0
    odd = jnp.logical_not(even)
    beside = has_prev.astype(jnp.int32) + has_next.astype(jnp.int32)
    barrier = pltpu.get_barrier_semaphore()

    def greet(sem, when):
        @pl.when(jnp.logical_and(when, has_next))
        def _():
            pl.semaphore_signal(sem, inc=1, device_id={"frame": frame + 1}, device_id_type=MESH)

        @pl.when(jnp.logical_and(when, has_prev))
        def _():
            pl.semaphore_signal(sem, inc=1, device_id={"frame": frame - 1}, device_id_type=MESH)

    pl.semaphore_signal(barrier, inc=1, device_id={"row": other}, device_id_type=MESH)
    greet(barrier, even)
    pl.semaphore_wait(barrier, jnp.where(odd, 1 + beside, 1))

    for i in range(2):
        row_copy(i, 0).start()

    greet(entered, odd)

    @pl.when(even)
    def _():
        pl.semaphore_wait(entered, beside)

    @pl.loop(0, half)
    def _(h):
        send_edges(h, 0)
        for i in range(3):
            local_copy(i, h).start()

    yields = lax.axis_index("head") == 1
    leaving = held.at[0, 0, 0:tile_frames]

    @pl.when(yields)
    def _():
        across(leaving, leaving, x_send.at[1], o_recv).wait_send()

    if half > 1:
        for i in range(2):
            row_copy(i, 1).start()

        @pl.when(yields)
        def _():
            across(leaving, leaving, x_send.at[1], o_recv).wait_send()

    @pl.loop(2, half)
    def _(h):
        for i in range(2):
            row_copy(i, h).start()

    @pl.loop(0, half)
    def _(h):
        row_copy(2, h).start()

    def attend(h, slot, j, first, count):
        q = held[2, h, 1 + j, slot]
        k = held[0, h, pl.ds(first, count)].reshape(-1, HD)
        v = held[1, h, pl.ds(first, count)].reshape(-1, HD)
        s = lax.dot_general(q, k, (((1,), (1,)), ((), ())), preferred_element_type=jnp.float32)
        m = jnp.max(s, axis=1, keepdims=True)
        p = jnp.exp2((s - m) * exponent_scale)
        l = jnp.sum(p, axis=1, keepdims=True)
        o = jnp.dot(p.astype(jnp.bfloat16), v, preferred_element_type=jnp.float32)
        obuf[h, j, slot] = (o / l).astype(obuf.dtype)

    @pl.loop(0, 2 * half)
    def _(step):
        remote = jnp.logical_and(step >= half - 1, step < 2 * half - 1)
        slot = remote.astype(jnp.int32)
        h = jnp.where(remote, step - half + 1, jnp.where(step < half, step, half - 1))

        @pl.when(step < half)
        def _():
            row_bytes(0, step).wait_recv()
            send_edges(step, 1)

        @pl.when(step == 0)
        def _():
            own = held.at[:, :, 1 : 1 + tile_frames, 0]
            pltpu.make_async_copy(own, own, local_sem).wait()
            receive_edges(0, 0)

        @pl.when(jnp.logical_or(step < half - 1, step == 2 * half - 2))
        def _():
            receive_edges(h, 1)

        @pl.when(remote)
        def _():
            row_bytes(1, h).wait_recv()

        @pl.loop(0, tile_frames)
        def _(j):
            below = jnp.logical_or(has_prev, j > 0)
            above = jnp.logical_or(has_next, j < tile_frames - 1)

            @pl.when(jnp.logical_and(below, above))
            def _():
                attend(h, slot, j, j, 3)

            @pl.when(jnp.logical_not(jnp.logical_and(below, above)))
            def _():
                attend(h, slot, j, jnp.where(below, j, j + 1), 2)

            @pl.when(slot == 1)
            def _():
                return_copy(h, j).start()

            @pl.when(slot == 0)
            def _():
                keep_copy(h, j).start()

    sent, returned = held.at[0, :, 0:tile_frames], obuf.at[:, :, 1]
    finish_edges()
    pltpu.make_async_copy(returned, returned, local_sem).wait()
    across(sent, sent, x_send.at[0], o_recv).wait_send()

    @pl.when(jnp.logical_not(yields))
    def _():
        across(sent, sent, x_send.at[1], o_recv).wait_send()

    if half > 2:
        later = held.at[0, 0 : half - 2, 0:tile_frames]

        @pl.when(yields)
        def _():
            across(later, later, x_send.at[1], o_recv).wait_send()

    across(returned, returned, x_send.at[0], o_recv).wait_recv()


def pair_attention(query, keys, values):
    tile_frames, tile_size, features = query.shape
    half = features // HD // 2
    kernel = functools.partial(
        pair_kernel,
        half=half,
        tile_frames=tile_frames,
        exponent_scale=math.log2(math.e) / math.sqrt(HD),
    )
    window = (3, half, tile_frames + 2, 2, tile_size, HD)
    own = (half, tile_frames, 2, tile_size, HD)
    dma = pltpu.SemaphoreType.DMA
    return pl.pallas_call(
        kernel,
        out_shape=jax.ShapeDtypeStruct(query.shape, query.dtype),
        in_specs=[pl.BlockSpec(memory_space=pltpu.HBM)] * 3,
        out_specs=pl.BlockSpec(memory_space=pltpu.VMEM),
        scratch_shapes=[
            pltpu.VMEM(window, query.dtype),
            pltpu.VMEM(own, query.dtype),
            dma,
            dma((2,)),
            dma((2, half)),
            dma,
            dma,
            dma((half,)),
            dma,
            pltpu.SemaphoreType.REGULAR,
        ],
        compiler_params=pltpu.CompilerParams(
            collective_id=0, has_side_effects=True, vmem_limit_bytes=40 * 1024 * 1024
        ),
    )(*(pltpu.with_memory_space_constraint(x, pltpu.HBM) for x in (query, keys, values)))


def shift(cells, axis, forward):
    count = lax.axis_size(axis)
    if forward:
        pairs = [(i, i + 1) for i in range(count - 1)]
    else:
        pairs = [(i + 1, i) for i in range(count - 1)]
    return lax.ppermute(cells, axis, pairs)


def attention_kernel(bias_ref, q_ref, k_ref, v_ref, o_ref, *, tile_frames, score_scale):
    for j in range(tile_frames):
        q = q_ref[j]
        k = k_ref[:, j : j + 3].reshape(-1, HD)
        v = v_ref[:, j : j + 3].reshape(-1, HD)
        s = lax.dot_general(q, k, (((1,), (1,)), ((), ())), preferred_element_type=jnp.float32)
        s = s * score_scale + bias_ref[j]
        m = jnp.max(s, axis=1, keepdims=True)
        p = jnp.exp(s - m)
        l = jnp.sum(p, axis=1, keepdims=True)
        o = jnp.dot(p.astype(jnp.bfloat16), v, preferred_element_type=jnp.float32)
        o_ref[j] = (o / l).astype(o_ref.dtype)


def per_device(query, keys, values):
    frames, rows, columns, features = query.shape
    tile_frames = frames // TF
    tile_size = TF * TR * TC
    heads_here = features // HD
    score_scale = 1.0 / math.sqrt(HD)

    def tiles(x):
        return x.reshape(tile_frames, tile_size, features)

    paired = lax.axis_size("row") == 2 and lax.axis_size("frame") > 1
    if paired and heads_here % 2 == 0 and tile_frames > 1:
        out = pair_attention(tiles(query), tiles(keys), tiles(values))
        return out.reshape(query.shape)

    kv = (tiles(keys), tiles(values))
    above = shift(kv, "row", True)
    below = shift(kv, "row", False)
    own_prev = shift(tuple(x[tile_frames - 1] for x in kv), "frame", True)
    own_next = shift(tuple(x[0] for x in kv), "frame", False)
    diag_prev = shift(
        tuple(jnp.stack((a[tile_frames - 1], b[tile_frames - 1])) for a, b in zip(above, below)),
        "frame",
        True,
    )
    diag_next = shift(tuple(jnp.stack((a[0], b[0])) for a, b in zip(above, below)), "frame", False)

    def window(i):
        middle = jnp.concatenate((own_prev[i][None], kv[i], own_next[i][None]), 0)
        top = jnp.concatenate((diag_prev[i][0][None], above[i], diag_next[i][0][None]), 0)
        bottom = jnp.concatenate((diag_prev[i][1][None], below[i], diag_next[i][1][None]), 0)
        return jnp.stack((top, middle, bottom))

    key_window = window(0)
    value_window = window(1)

    frame_index = lax.axis_index("frame")
    row_index = lax.axis_index("row")
    offsets = jnp.arange(3, dtype=jnp.int32) - 1
    global_frames = frame_index * tile_frames + jnp.arange(tile_frames + 2, dtype=jnp.int32) - 1
    frame_ok = (global_frames >= 0) & (global_frames < tile_frames * lax.axis_size("frame"))
    row_ids = row_index + offsets
    row_ok = (row_ids >= 0) & (row_ids < lax.axis_size("row"))
    bias_rows = []
    for j in range(tile_frames):
        ok = row_ok[:, None] & frame_ok[None, j : j + 3]
        ok = jnp.broadcast_to(ok[:, :, None], (3, 3, tile_size)).reshape(1, 9 * tile_size)
        bias_rows.append(jnp.where(ok, 0.0, -jnp.inf).astype(jnp.float32))
    bias = jnp.stack(bias_rows)

    q = tiles(query)
    kernel = functools.partial(
        attention_kernel, tile_frames=tile_frames, score_scale=score_scale
    )
    window_block = (3, tile_frames + 2, tile_size, HD)
    out = pl.pallas_call(
        kernel,
        grid=(heads_here,),
        in_specs=[
            pl.BlockSpec((tile_frames, 1, 9 * tile_size), lambda h: (0, 0, 0)),
            pl.BlockSpec((tile_frames, tile_size, HD), lambda h: (0, 0, h)),
            pl.BlockSpec(window_block, lambda h: (0, 0, 0, h)),
            pl.BlockSpec(window_block, lambda h: (0, 0, 0, h)),
        ],
        out_specs=pl.BlockSpec((tile_frames, tile_size, HD), lambda h: (0, 0, h)),
        out_shape=jax.ShapeDtypeStruct(q.shape, query.dtype),
        compiler_params=pltpu.CompilerParams(vmem_limit_bytes=48 * 1024 * 1024),
    )(bias, q, key_window, value_window)
    return out.reshape(frames, rows, columns, features)


def solution(mesh):
    return jax.shard_map(
        per_device,
        mesh=mesh,
        in_specs=(
            P(("clips", "frame"), "row", None, "head"),
            P(("clips", "frame"), "row", None, "head"),
            P(("clips", "frame"), "row", None, "head"),
        ),
        out_specs=P(("clips", "frame"), "row", None, "head"),
        check_vma=False,
    )
```

```python
import functools
import math

import jax
import jax.numpy as jnp
from jax import lax
from jax.experimental import pallas as pl
from jax.experimental.pallas import tpu as pltpu
from jax.sharding import PartitionSpec as P

HD = 128
TF = 4
TR = 8
TC = 8
MESH = pl.DeviceIdType.MESH


def pair_kernel(
    q_ref,
    k_ref,
    v_ref,
    o_ref,
    held,
    obuf,
    local_sem,
    x_send,
    x_recv,
    z_send,
    z_recv,
    f_recv,
    o_recv,
    entered,
    *,
    half,
    tile_frames,
    exponent_scale,
):
    row = lax.axis_index("row")
    frame = lax.axis_index("frame")
    clip = lax.axis_index("clips")
    head = lax.axis_index("head")
    last_frame = lax.axis_size("frame") - 1
    other = 1 - row
    has_prev = frame > 0
    has_next = frame < last_frame
    sources = (k_ref, v_ref, q_ref)


    def columns(side, h):
        return pl.ds(pl.multiple_of((side * half + h) * HD, HD), HD)

    def place(i, h, slot):
        return held.at[i, h, 1 : 1 + tile_frames, slot]

    def local_copy(i, h):
        return pltpu.make_async_copy(
            sources[i].at[:, :, columns(row, h)], place(i, h, 0), local_sem
        )

    def across(source, target, send_sem, recv_sem):
        return pltpu.make_async_remote_copy(
            source, target, send_sem, recv_sem, device_id=(clip, frame, other, head), device_id_type=MESH
        )

    def along(source, target, send_sem, recv_sem, up):
        device = (clip, frame + 1 if up else frame - 1, row, head)
        return pltpu.make_async_remote_copy(
            source, target, send_sem, recv_sem, device_id=device, device_id_type=MESH
        )

    def row_copy(i, h, first=0):
        kind = i // 2
        sem = x_send.at[0 if kind else first or 2]
        source = sources[i].at[:, :, columns(other, h)]
        return across(source, place(i, h, 1), sem, x_recv.at[kind, h])

    def row_bytes(kind, h):
        whole = held.at[2, h, 0:tile_frames, 1] if kind else held.at[0, h, 0:tile_frames]
        return across(whole, whole, x_send.at[0], x_recv.at[kind, h])

    def send_edges(h, slot):
        for up in (True, False):

            @pl.when(has_next if up else has_prev)
            def _():
                for i in range(2):
                    edge = tile_frames - 1 if up else 0
                    target = held.at[i, h, 0 if up else tile_frames + 1, slot]
                    if slot == 0:
                        source, recv = sources[i].at[edge, :, columns(row, h)], z_recv
                    else:
                        source, recv = held.at[i, h, 1 + edge, 1], f_recv.at[h]
                    along(source, target, z_send, recv, up).start()

    def by_neighbours(one, two, wait):
        both = jnp.logical_and(has_prev, has_next)

        @pl.when(both)
        def _():
            wait(two)

        @pl.when(jnp.logical_not(both))
        def _():
            wait(one)

    def receive_edges(h, slot):
        one = held.at[0, :, 0] if slot == 0 else held.at[0, h, 0]
        two = held.at[0, :, 0:2] if slot == 0 else held.at[0, h, 0:2]
        recv = z_recv if slot == 0 else f_recv.at[h]
        by_neighbours(one, two, lambda whole: across(whole, whole, z_send, recv).wait_recv())

    def finish_edges():
        one, two = held.at[0, :, 0:2], held.at[0:2, :, 0:2]
        by_neighbours(one, two, lambda whole: across(whole, whole, z_send, z_recv).wait_send())

    def return_copy(h, j):
        return across(obuf.at[h, j, 1], o_ref.at[j, :, columns(row, h)], x_send.at[0], o_recv)

    def keep_copy(h, j):
        return pltpu.make_async_copy(
            obuf.at[h, j, 0], o_ref.at[j, :, columns(row, h)], local_sem
        )

    even = lax.rem(frame, 2) == 0
    odd = jnp.logical_not(even)
    beside = has_prev.astype(jnp.int32) + has_next.astype(jnp.int32)
    barrier = pltpu.get_barrier_semaphore()

    def greet(sem, when):
        @pl.when(jnp.logical_and(when, has_next))
        def _():
            pl.semaphore_signal(sem, inc=1, device_id=(clip, frame + 1, row, head), device_id_type=MESH)

        @pl.when(jnp.logical_and(when, has_prev))
        def _():
            pl.semaphore_signal(sem, inc=1, device_id=(clip, frame - 1, row, head), device_id_type=MESH)

    pl.semaphore_signal(barrier, inc=1, device_id=(clip, frame, other, head), device_id_type=MESH)
    greet(barrier, even)
    pl.semaphore_wait(barrier, jnp.where(odd, 1 + beside, 1))

    for i in range(2):
        row_copy(i, 0, 1).start()

    greet(entered, odd)

    @pl.when(even)
    def _():
        pl.semaphore_wait(entered, beside)

    @pl.loop(0, half)
    def _(h):
        send_edges(h, 0)
        for i in range(3):
            local_copy(i, h).start()

    yields = head == 1
    leaving = held.at[0, 0, 0:tile_frames]

    @pl.when(yields)
    def _():
        across(leaving, leaving, x_send.at[1], o_recv).wait_send()

    if half > 1:
        for i in range(2):
            row_copy(i, 1, 3).start()

        @pl.when(yields)
        def _():
            across(leaving, leaving, x_send.at[3], o_recv).wait_send()

    @pl.loop(2, half)
    def _(h):
        for i in range(2):
            row_copy(i, h).start()

    @pl.loop(0, half)
    def _(h):
        row_copy(2, h).start()

    def attend(h, slot, j, first, count):
        q = held[2, h, 1 + j, slot]
        k = held[0, h, pl.ds(first, count)].reshape(-1, HD)
        v = held[1, h, pl.ds(first, count)].reshape(-1, HD)
        s = lax.dot_general(q, k, (((1,), (1,)), ((), ())), preferred_element_type=jnp.float32)
        m = jnp.max(s, axis=1, keepdims=True)
        p = jnp.exp2((s - m) * exponent_scale)
        l = jnp.sum(p, axis=1, keepdims=True)
        o = jnp.dot(p.astype(jnp.bfloat16), v, preferred_element_type=jnp.float32)
        obuf[h, j, slot] = (o / l).astype(obuf.dtype)

    @pl.loop(0, 2 * half)
    def _(step):
        remote = jnp.logical_and(step >= half - 1, step < 2 * half - 1)
        slot = remote.astype(jnp.int32)
        h = jnp.where(remote, step - half + 1, jnp.where(step < half, step, half - 1))

        @pl.when(step < half)
        def _():
            row_bytes(0, step).wait_recv()
            send_edges(step, 1)

        @pl.when(step == 0)
        def _():
            own = held.at[:, :, 1 : 1 + tile_frames, 0]
            pltpu.make_async_copy(own, own, local_sem).wait()
            receive_edges(0, 0)

        @pl.when(jnp.logical_or(step < half - 1, step == 2 * half - 2))
        def _():
            receive_edges(h, 1)

        @pl.when(remote)
        def _():
            row_bytes(1, h).wait_recv()

        @pl.loop(0, tile_frames)
        def _(j):
            below = jnp.logical_or(has_prev, j > 0)
            above = jnp.logical_or(has_next, j < tile_frames - 1)

            @pl.when(jnp.logical_and(below, above))
            def _():
                attend(h, slot, j, j, 3)

            @pl.when(jnp.logical_not(jnp.logical_and(below, above)))
            def _():
                attend(h, slot, j, jnp.where(below, j, j + 1), 2)

            @pl.when(slot == 1)
            def _():
                return_copy(h, j).start()

            @pl.when(slot == 0)
            def _():
                keep_copy(h, j).start()

    sent, returned = held.at[0, :, 0:tile_frames], obuf.at[:, :, 1]
    finish_edges()
    pltpu.make_async_copy(returned, returned, local_sem).wait()
    across(sent, sent, x_send.at[0], o_recv).wait_send()

    @pl.when(jnp.logical_not(yields))
    def _():
        across(leaving, leaving, x_send.at[1], o_recv).wait_send()
        if half > 1:
            across(leaving, leaving, x_send.at[3], o_recv).wait_send()

    if half > 2:
        later = held.at[0, 0 : half - 2, 0:tile_frames]
        across(later, later, x_send.at[2], o_recv).wait_send()
    across(returned, returned, x_send.at[0], o_recv).wait_recv()


def pair_attention(query, keys, values):
    tile_frames, tile_size, features = query.shape
    half = features // HD // 2
    kernel = functools.partial(
        pair_kernel,
        half=half,
        tile_frames=tile_frames,
        exponent_scale=math.log2(math.e) / math.sqrt(HD),
    )
    window = (3, half, tile_frames + 2, 2, tile_size, HD)
    own = (half, tile_frames, 2, tile_size, HD)
    dma = pltpu.SemaphoreType.DMA
    return pl.pallas_call(
        kernel,
        out_shape=jax.ShapeDtypeStruct(query.shape, query.dtype),
        in_specs=[pl.BlockSpec(memory_space=pltpu.HBM)] * 3,
        out_specs=pl.BlockSpec(memory_space=pltpu.VMEM),
        scratch_shapes=[
            pltpu.VMEM(window, query.dtype),
            pltpu.VMEM(own, query.dtype),
            dma,
            dma((4,)),
            dma((2, half)),
            dma,
            dma,
            dma((half,)),
            dma,
            pltpu.SemaphoreType.REGULAR,
        ],
        compiler_params=pltpu.CompilerParams(
            collective_id=0, has_side_effects=True, vmem_limit_bytes=40 * 1024 * 1024
        ),
    )(*(pltpu.with_memory_space_constraint(x, pltpu.HBM) for x in (query, keys, values)))


def shift(cells, axis, forward):
    count = lax.axis_size(axis)
    if forward:
        pairs = [(i, i + 1) for i in range(count - 1)]
    else:
        pairs = [(i + 1, i) for i in range(count - 1)]
    return lax.ppermute(cells, axis, pairs)


def attention_kernel(bias_ref, q_ref, k_ref, v_ref, o_ref, *, tile_frames, score_scale):
    for j in range(tile_frames):
        q = q_ref[j]
        k = k_ref[:, j : j + 3].reshape(-1, HD)
        v = v_ref[:, j : j + 3].reshape(-1, HD)
        s = lax.dot_general(q, k, (((1,), (1,)), ((), ())), preferred_element_type=jnp.float32)
        s = s * score_scale + bias_ref[j]
        m = jnp.max(s, axis=1, keepdims=True)
        p = jnp.exp(s - m)
        l = jnp.sum(p, axis=1, keepdims=True)
        o = jnp.dot(p.astype(jnp.bfloat16), v, preferred_element_type=jnp.float32)
        o_ref[j] = (o / l).astype(o_ref.dtype)


def per_device(query, keys, values):
    frames, rows, columns, features = query.shape
    tile_frames = frames // TF
    tile_size = TF * TR * TC
    heads_here = features // HD
    score_scale = 1.0 / math.sqrt(HD)

    def tiles(x):
        return x.reshape(tile_frames, tile_size, features)

    paired = lax.axis_size("row") == 2 and lax.axis_size("frame") > 1
    if paired and heads_here % 2 == 0 and tile_frames > 1:
        out = pair_attention(tiles(query), tiles(keys), tiles(values))
        return out.reshape(query.shape)

    kv = (tiles(keys), tiles(values))
    above = shift(kv, "row", True)
    below = shift(kv, "row", False)
    own_prev = shift(tuple(x[tile_frames - 1] for x in kv), "frame", True)
    own_next = shift(tuple(x[0] for x in kv), "frame", False)
    diag_prev = shift(
        tuple(jnp.stack((a[tile_frames - 1], b[tile_frames - 1])) for a, b in zip(above, below)),
        "frame",
        True,
    )
    diag_next = shift(tuple(jnp.stack((a[0], b[0])) for a, b in zip(above, below)), "frame", False)

    def window(i):
        middle = jnp.concatenate((own_prev[i][None], kv[i], own_next[i][None]), 0)
        top = jnp.concatenate((diag_prev[i][0][None], above[i], diag_next[i][0][None]), 0)
        bottom = jnp.concatenate((diag_prev[i][1][None], below[i], diag_next[i][1][None]), 0)
        return jnp.stack((top, middle, bottom))

    key_window = window(0)
    value_window = window(1)

    frame_index = lax.axis_index("frame")
    row_index = lax.axis_index("row")
    offsets = jnp.arange(3, dtype=jnp.int32) - 1
    global_frames = frame_index * tile_frames + jnp.arange(tile_frames + 2, dtype=jnp.int32) - 1
    frame_ok = (global_frames >= 0) & (global_frames < tile_frames * lax.axis_size("frame"))
    row_ids = row_index + offsets
    row_ok = (row_ids >= 0) & (row_ids < lax.axis_size("row"))
    bias_rows = []
    for j in range(tile_frames):
        ok = row_ok[:, None] & frame_ok[None, j : j + 3]
        ok = jnp.broadcast_to(ok[:, :, None], (3, 3, tile_size)).reshape(1, 9 * tile_size)
        bias_rows.append(jnp.where(ok, 0.0, -jnp.inf).astype(jnp.float32))
    bias = jnp.stack(bias_rows)

    q = tiles(query)
    kernel = functools.partial(
        attention_kernel, tile_frames=tile_frames, score_scale=score_scale
    )
    window_block = (3, tile_frames + 2, tile_size, HD)
    out = pl.pallas_call(
        kernel,
        grid=(heads_here,),
        in_specs=[
            pl.BlockSpec((tile_frames, 1, 9 * tile_size), lambda h: (0, 0, 0)),
            pl.BlockSpec((tile_frames, tile_size, HD), lambda h: (0, 0, h)),
            pl.BlockSpec(window_block, lambda h: (0, 0, 0, h)),
            pl.BlockSpec(window_block, lambda h: (0, 0, 0, h)),
        ],
        out_specs=pl.BlockSpec((tile_frames, tile_size, HD), lambda h: (0, 0, h)),
        out_shape=jax.ShapeDtypeStruct(q.shape, query.dtype),
        compiler_params=pltpu.CompilerParams(vmem_limit_bytes=48 * 1024 * 1024),
    )(bias, q, key_window, value_window)
    return out.reshape(frames, rows, columns, features)


def solution(mesh):
    return jax.shard_map(
        per_device,
        mesh=mesh,
        in_specs=(
            P(("clips", "frame"), "row", None, "head"),
            P(("clips", "frame"), "row", None, "head"),
            P(("clips", "frame"), "row", None, "head"),
        ),
        out_specs=P(("clips", "frame"), "row", None, "head"),
        check_vma=False,
    )
```
